512 devices in a mesh: rows: 64 (over x, y, core), feat: 8 (over z).
Axes of the slice: x: 4, y: 8, z: 8, core: 2. Of those that a mesh axis runs over, the one named last changes fastest.
Arguments:
- scores: float32 [131072], P(('rows', 'feat')), may hold values from -6 to 6
- weights: float32 [131072], P(('rows', 'feat')), may hold values from 0.25 to 4
- labels: int32 [131072], P(('rows', 'feat')), may hold values from 0 to 4
- owner_row: int32 [131072], P(('rows', 'feat')), may hold values from 0 to 63, as said below
- owner_slot: int32 [131072], P(('rows', 'feat')), may hold values from 0 to 255, as said below
- query_len: int32 [512, 4], P(('rows', 'feat')), may hold values from 1 to 128, 256 in all within a row
- bin_index: int32 [512, 131072], P('feat', 'rows'), may hold values from 0 to 255
- parent: int32 [131072], P('rows'), may hold values from 0 to 15, as said below
- split_feat: int32 [16], replicated, may hold values from 0 to 511
- split_thr: int32 [16], replicated, may hold values from 0 to 254
Outputs:
- histogram: float32 [64, 512, 256], P('rows', 'feat')
- new_node: int32 [131072], P(('rows', 'feat'))
The draws below stay inside these ranges and needn't reach their ends.
Inputs may be any that keep to these rules, and one draw needn't show every extreme that they name: `owner_row`: documents move only along rows: an owner keeps the sender's feat index. One device holds at most 8 documents of one owner, exactly 8 for some device and owner in every draw, and every owner owns exactly 256 documents. The documents of one owner carry distinct owner_slot values, each of 0 to 255 once. The lengths in one row of query_len sum to 256. Among the documents of one index of rows, each parent node holds at most 160, and some parent holds exactly 160 in every index of rows.
All inputs are finite; a program needn't handle non-finite values.
Results may differ from the reference program's by a relative error of at most 0.0028.
Values may be sent and summed in bfloat16 or wider, within the bound.
No kernel may reach another device: no remote copies, remote signals or barrier semaphores. Data moves between devices by JAX's collectives and lax.ppermute only.
A program may use at most 64 MiB of HBM per device.

```python
import math
import jax
import jax.numpy as jnp
import numpy as np
from jax import lax

F = 512
BINS = 256
NODES = 32
QMAX = 128
DOC_DEV = 256
PARENTS = 16
Q_OWN = 4
DOCS = 131072
N_ROWS = 64
N_FEAT = 8
DEVICES = 512


def routing_plan(key):
    half_slot = DOC_DEV // N_ROWS
    column_total = N_ROWS * DOC_DEV

    def one_column(column_key):
        pair_key, move_key, slot_key, order_key = jax.random.split(column_key, 4)
        offset_order = jax.random.permutation(pair_key, N_ROWS)
        moved = jax.random.randint(move_key, (N_ROWS // 2,), 0, half_slot + 1)
        moved = moved.at[0].set(half_slot)
        counts = jnp.full((N_ROWS,), half_slot, jnp.int32)
        counts = counts.at[offset_order[0::2]].add(moved).at[offset_order[1::2]].add(-moved)
        bounds = jnp.cumsum(counts)
        places = jnp.arange(DOC_DEV, dtype=jnp.int32)
        offsets = jnp.sum((places[:, None] >= bounds[None, :]).astype(jnp.int32), axis=1)
        owners = jnp.arange(N_ROWS, dtype=jnp.int32)
        homes = (owners[:, None] + offsets[None, :]) % N_ROWS
        slot_keys = jax.random.split(slot_key, N_ROWS)
        slots = jax.vmap(lambda single: jax.random.permutation(single, DOC_DEV))(slot_keys)
        shuffle = jax.random.permutation(order_key, column_total)
        sort_key = homes.reshape(-1) * column_total + shuffle
        arranged = jnp.argsort(sort_key, stable=True)
        owner_ids = jnp.repeat(owners, DOC_DEV)[arranged]
        slot_ids = slots.reshape(-1)[arranged]
        return (owner_ids.reshape(N_ROWS, DOC_DEV), slot_ids.reshape(N_ROWS, DOC_DEV))
    column_keys = jax.random.split(jax.random.fold_in(key, 7031), N_FEAT)
    owner_ids, slot_ids = jax.vmap(one_column)(column_keys)
    owner_ids = jnp.transpose(owner_ids, (1, 0, 2)).reshape(-1).astype(jnp.int32)
    slot_ids = jnp.transpose(slot_ids, (1, 0, 2)).reshape(-1).astype(jnp.int32)
    return (owner_ids, slot_ids)


def draw_owner_row(key, part):
    return routing_plan(key)[0]


def draw_owner_slot(key, part):
    return routing_plan(key)[1]


def draw_labels(key, part):
    grade_key, keep_key = jax.random.split(jax.random.fold_in(key, 4409))
    grade = jax.random.randint(grade_key, (DOCS,), 0, 5)
    keeper = (jax.random.randint(keep_key, (DOCS,), 0, 4) == 0).astype(jnp.int32)
    return (grade * keeper).astype(jnp.int32)


def draw_parent(key, part):
    group_docs = N_FEAT * DOC_DEV
    mean_count = group_docs // PARENTS
    spread = mean_count // 4

    def one_group(group_key):
        pair_key, move_key, place_key = jax.random.split(group_key, 3)
        order = jax.random.permutation(pair_key, PARENTS)
        moved = jax.random.randint(move_key, (PARENTS // 2,), 0, spread + 1)
        moved = moved.at[0].set(spread)
        counts = jnp.full((PARENTS,), mean_count, jnp.int32)
        counts = counts.at[order[0::2]].add(moved).at[order[1::2]].add(-moved)
        bounds = jnp.cumsum(counts)
        places = jnp.arange(group_docs, dtype=jnp.int32)
        node_ids = jnp.sum((places[:, None] >= bounds[None, :]).astype(jnp.int32), axis=1)
        return node_ids[jax.random.permutation(place_key, group_docs)]
    group_keys = jax.random.split(jax.random.fold_in(key, 5813), N_ROWS)
    return jax.vmap(one_group)(group_keys).reshape(-1).astype(jnp.int32)


def set_ends(drawn, own_key, low, top_value):
    index_at = [jax.random.randint(jax.random.fold_in(own_key, axis), (), 0, length) for axis, length in enumerate(drawn.shape)]
    widest = drawn.shape.index(max(drawn.shape))
    beside = index_at[:widest] + [(index_at[widest] + 1) % drawn.shape[widest]] + index_at[widest + 1:]
    return drawn.at[tuple(index_at)].set(low).at[tuple(beside)].set(top_value)


def block_scale(key, extent, cuts, low, top_value):
    loudness = 1.0
    for axis_at, parts in cuts:
        heights = jax.random.uniform(jax.random.fold_in(jax.random.fold_in(key, 6), axis_at), (parts,), jnp.float32, low / len(cuts), top_value / len(cuts))
        loudness = loudness * jnp.repeat(jnp.exp(heights), extent[axis_at] // parts).reshape((-1,) + (1,) * (len(extent) - 1 - axis_at))
    return loudness


def profile(number_of, total, bound, skew):
    loads = [(1 << 20) // math.isqrt(rank ** skew) + 1 for rank in range(2, number_of + 1)]
    surplus, holding = total - bound - (number_of - 1), [1] * (number_of - 1)
    while surplus > 0:
        movable = [i for i in range(number_of - 1) if holding[i] < bound]
        whole, left = sum([loads[i] for i in movable]), surplus
        for i in movable:
            more = min(bound - holding[i], max(1, left * loads[i] // whole), surplus)
            holding[i] = holding[i] + more
            surplus = surplus - more
    return np.array([bound] + holding)


def ragged_sizes(own_key, number_of, total, limit, skew):
    if number_of == 2:
        one = jax.random.randint(own_key, (), max(1, total - limit), min(limit, total - 1) + 1)
        return jnp.stack([one, total - one])
    sizes = jnp.asarray(profile(number_of, total, limit, skew), jnp.int32)
    pairs = (number_of - 1) // 2
    donor, receiver = sizes[1:1 + 2 * pairs:2], sizes[2:2 + 2 * pairs:2]
    slack = jnp.minimum(donor - 1, limit - receiver)
    moved = jax.random.randint(jax.random.fold_in(own_key, 1), (pairs,), 0, 1 << 20) % (slack + 1)
    sizes = sizes.at[1:1 + 2 * pairs:2].set(donor - moved).at[2:2 + 2 * pairs:2].set(receiver + moved)
    return sizes[jax.random.permutation(jax.random.fold_in(own_key, 2), number_of)]


def noise(own_key, extent, deviation, most, shards=(), kind=jnp.bfloat16):
    result = jax.random.normal(own_key, extent, jnp.float32) * deviation
    if len(shards) > 0:
        result = block_scale(own_key, extent, shards, -0.22, 0.18) * result
    return jnp.clip(result, min=-most, max=most).astype(kind)


def setup_inputs(seed: int = 0) -> dict:
    keys = jax.random.split(jax.random.key(seed), 11)
    return {
        "scores": noise(keys[0], (DOCS,), 1.5, 6.0, ((0, 512),), jnp.float32),
        "weights": jnp.clip(jnp.exp(math.log(4.0) - 2.7725887 * jax.random.uniform(keys[1], (DOCS,), jnp.float32) ** block_scale(keys[1], (DOCS,), ((0, 512),), -0.2, 0.2)), 0.25, 4.0),
        "labels": draw_labels(jax.random.fold_in(keys[10], 71), 0),
        "owner_row": draw_owner_row(jax.random.fold_in(keys[10], 71), 0),
        "owner_slot": draw_owner_slot(jax.random.fold_in(keys[10], 71), 0),
        "query_len": jax.vmap(lambda own: ragged_sizes(own, Q_OWN, DOC_DEV, QMAX, 2))(jax.random.split(keys[5], DEVICES)).reshape((DEVICES, Q_OWN)).astype(jnp.int32),
        "bin_index": set_ends(jax.random.randint(keys[6], (F, DOCS), 0, BINS), jax.random.fold_in(keys[6], 1), 0, BINS - 1).astype(jnp.int32),
        "parent": draw_parent(jax.random.fold_in(keys[10], 71), 0),
        "split_feat": set_ends(jax.random.randint(keys[8], (PARENTS,), 0, F), jax.random.fold_in(keys[8], 1), 0, F - 1).astype(jnp.int32),
        "split_thr": set_ends(jax.random.randint(keys[9], (PARENTS,), 0, BINS - 1), jax.random.fold_in(keys[9], 1), 0, (BINS - 1) - 1).astype(jnp.int32),
    }


sigma_scale = 1.0


def query_lambdas(doc_score, weight, doc_label, usable):
    usable_f = usable.astype(jnp.float32)
    doc_gain = (jnp.exp2(doc_label.astype(jnp.float32)) - 1.0) * usable_f
    places = jnp.arange(doc_score.shape[1], dtype=jnp.int32)
    ranked_above = (doc_score[:, None, :] > doc_score[:, :, None]) | ((doc_score[:, None, :] == doc_score[:, :, None]) & (places[None, None, :] < places[None, :, None]))
    doc_rank = 1.0 + jnp.sum(ranked_above.astype(jnp.float32) * usable_f[:, None, :], axis=2)
    discount = 1.0 / jnp.log2(1.0 + doc_rank)
    levels = jnp.arange(1, 5, dtype=jnp.int32)
    counts = jnp.sum(((doc_label[:, :, None] >= levels[None, None, :]) & usable[:, :, None]).astype(jnp.int32), axis=1)
    ideal_label = jnp.sum((places[None, :, None] < counts[:, None, :]).astype(jnp.int32), axis=2)
    ideal_gain = jnp.exp2(ideal_label.astype(jnp.float32)) - 1.0
    ideal_dcg = jnp.sum(ideal_gain / jnp.log2(places.astype(jnp.float32) + 2.0)[None, :], axis=1)
    inv_ideal = 1.0 / jnp.maximum(ideal_dcg, 1.0)
    swap_gain = jnp.abs(doc_gain[:, :, None] - doc_gain[:, None, :]) * jnp.abs(discount[:, :, None] - discount[:, None, :])
    swap_gain = swap_gain * (weight[:, :, None] * weight[:, None, :]) * inv_ideal[:, None, None]
    better = ((doc_label[:, :, None] > doc_label[:, None, :]) & usable[:, :, None] & usable[:, None, :]).astype(jnp.float32)
    misorder = jax.nn.sigmoid(-sigma_scale * (doc_score[:, :, None] - doc_score[:, None, :]))
    pushed = better * misorder * swap_gain
    gradient = sigma_scale * (jnp.sum(pushed, axis=1) - jnp.sum(pushed, axis=2))
    curvature = (better + jnp.swapaxes(better, 1, 2)) * misorder * (1.0 - misorder) * swap_gain
    hessian = sigma_scale * sigma_scale * jnp.sum(curvature, axis=2)
    return gradient, hessian


def owner_lambdas(doc_score, weight, doc_label, lengths):
    doc_count = doc_score.shape[0]
    starts = jnp.cumsum(lengths) - lengths
    places = jnp.arange(QMAX, dtype=jnp.int32)
    flat_index = (starts[:, None] + places[None, :]).astype(jnp.int32)
    usable = places[None, :] < lengths[:, None]
    clipped = jnp.clip(flat_index, 0, doc_count - 1)
    gradient, hessian = query_lambdas(doc_score[clipped], weight[clipped], jnp.where(usable, doc_label[clipped], 0), usable)
    target = jnp.where(usable, flat_index, doc_count).reshape(-1)
    grad_flat = jnp.zeros((doc_count + 1,), jnp.float32).at[target].set(gradient.reshape(-1))[:doc_count]
    hess_flat = jnp.zeros((doc_count + 1,), jnp.float32).at[target].set(hessian.reshape(-1))[:doc_count]
    return grad_flat, hess_flat


def reference(scores, weights, labels, owner_row, owner_slot, query_len, bin_index, parent, split_feat, split_thr):
    devices_all = N_ROWS * N_FEAT
    doc_ids = jnp.arange(DOCS, dtype=jnp.int32)
    column = (doc_ids // DOC_DEV) % N_FEAT
    target = ((owner_row * N_FEAT + column) * DOC_DEV + owner_slot).astype(jnp.int32)
    source = jnp.zeros((DOCS,), jnp.int32).at[target].set(doc_ids)
    owner_data = (scores[source].reshape(devices_all, DOC_DEV), weights[source].reshape(devices_all, DOC_DEV), labels[source].reshape(devices_all, DOC_DEV), query_len)
    gradient, hessian = lax.map(lambda packed: owner_lambdas(packed[0], packed[1], packed[2], packed[3]), owner_data)
    grad_b = gradient.reshape(-1)[target].astype(jnp.bfloat16)
    hess_b = hessian.reshape(-1)[target].astype(jnp.bfloat16)
    chosen = split_feat[parent]
    picked = bin_index[chosen, doc_ids]
    went_right = (picked > split_thr[parent]).astype(jnp.int32)
    new_node = 2 * parent + went_right
    group_width = F // N_FEAT

    def tally_stat(values):
        pieces = []
        for part_index in range(N_FEAT):
            group_bins = bin_index[part_index * group_width:(part_index + 1) * group_width]
            cell_ids = new_node[None, :] * (group_width * BINS) + jnp.arange(group_width, dtype=jnp.int32)[:, None] * BINS + group_bins
            spread = jnp.broadcast_to(values[None, :], (group_width, DOCS))
            summed = jax.ops.segment_sum(spread.reshape(-1), cell_ids.reshape(-1), num_segments=NODES * group_width * BINS)
            pieces.append(summed.reshape(NODES, group_width, BINS))
        return jnp.concatenate(pieces, axis=1)

    histogram = jnp.concatenate([tally_stat(grad_b.astype(jnp.float32)), tally_stat(hess_b.astype(jnp.float32))], axis=0)
    return histogram, new_node
```

```python
import functools

import jax
import jax.numpy as jnp
from jax import lax
from jax.experimental import pallas as pl
from jax.experimental.pallas import tpu as pltpu
from jax.sharding import PartitionSpec as P

BINS = 256
NODES = 32
QMAX = 128
PARENTS = 16
ROWS = 64
FEATS = 8
DOC = 256
GROUP = FEATS * DOC
SPAN = 64
CAP = 160
SLOTS = PARENTS * CAP
POS = 8
PEERS = 16
TAKEN = PEERS * CAP
TILES = TAKEN // 128
CHUNK = 88
SHARE = 64

F32 = jnp.float32
BF16 = jnp.bfloat16
I32 = jnp.int32


def iota(shape, dim):
    return lax.broadcasted_iota(I32, shape, dim)


def nt(a, b):
    return lax.dot_general(a, b, (((1,), (1,)), ((), ())), preferred_element_type=F32)


def nn(a, b):
    return jnp.dot(a, b, preferred_element_type=F32)


def as_hot(mask):
    return jnp.where(mask, 1.0, 0.0).astype(BF16)


def three_parts(x):
    top = x.astype(BF16).astype(F32)
    rest = x - top
    middle = rest.astype(BF16).astype(F32)
    return top, middle, rest - middle


def swap_matrix():
    row = iota((512, 1), 0)
    goal = ((row >> 5) & 3) * 128 + (row >> 7) * 32 + (row & 31)
    return as_hot(goal == iota((512, 512), 1))


def earlier_matrix():
    return as_hot(iota((DOC, DOC), 0) < iota((DOC, DOC), 1))


def stack_rows(rows, height, width):
    place = iota((height, width), 0)
    out = jnp.zeros((height, width), F32)
    for at, row in enumerate(rows):
        out = jnp.where(place == at, row, out)
    return out


def send_kernel(score_ref, weight_ref, label_ref, owner_ref, slot_ref, out_ref):
    owner = owner_ref[...]
    hot = jnp.where(iota((ROWS, DOC), 0) == owner, 1.0, 0.0)
    before = nn(hot.astype(BF16), earlier_matrix())
    place = jnp.sum(hot * before, axis=0, keepdims=True)
    rows = [
        *three_parts(score_ref[...]),
        *three_parts(weight_ref[...]),
        slot_ref[...].astype(F32) + 1.0,
        label_ref[...].astype(F32),
    ]
    values = stack_rows(rows, 16, DOC)
    tiled = jnp.concatenate([values] * POS, axis=0)
    group = iota((16 * POS, DOC), 0) >> 4
    total = jnp.zeros((ROWS, 128), F32)
    for pos in range(POS):
        here = jnp.where(place == float(pos), hot, 0.0).astype(BF16)
        total += nt(here, jnp.where(group == pos, tiled, 0.0).astype(BF16))
    out_ref[:, 0, :] = total


def owner_kernel(len_ref, in_ref, out_ref):
    data = in_ref[:, 0, :]
    turned = jnp.transpose(data).astype(BF16)
    lane = iota((ROWS, DOC), 1).astype(F32) + 1.0
    table = jnp.zeros((16, DOC), F32)
    for pos in range(POS):
        hot = as_hot(data[:, pos * 16 + 6 : pos * 16 + 7] == lane)
        table += nn(turned[pos * 16 : pos * 16 + 16, :], hot)
    same = as_hot(iota((DOC, DOC), 0) == iota((DOC, DOC), 1))
    upright = nt(same, table.astype(BF16))
    s_j = table[0:1] + table[1:2] + table[2:3]
    w_j = table[3:4] + table[4:5] + table[5:6]
    l_j = table[7:8]
    s_i = upright[:, 0:1] + upright[:, 1:2] + upright[:, 2:3]
    w_i = upright[:, 3:4] + upright[:, 4:5] + upright[:, 5:6]
    l_i = upright[:, 7:8]

    ends = []
    total = 0
    for q in range(3):
        total = total + len_ref[0, q]
        ends.append(total)

    def query_of(at):
        return sum([(at >= end).astype(I32) for end in ends])

    def gain(label):
        return sum([jnp.where(label >= float(l), 2.0 ** (l - 1), 0.0) for l in range(1, 5)])

    row_at = iota((1, DOC), 1)
    q_j = query_of(row_at)
    q_i = query_of(iota((DOC, 1), 0))
    n_j = jnp.zeros((1, DOC), F32)
    for q in range(4):
        n_j = jnp.where(q_j == q, len_ref[0, q].astype(F32), n_j)

    case = iota((16, DOC), 0)
    level = ((case & 3) + 1).astype(F32)
    reaches = (q_j == (case >> 2)) & (l_j >= level)
    count = jnp.sum(jnp.where(reaches, 1.0, 0.0), axis=1, keepdims=True)
    spot = iota((16, QMAX), 1).astype(F32)
    step = jnp.left_shift(1, iota((16, QMAX), 0) & 3).astype(F32)
    share = jnp.where(spot < count, step * (0.6931471805599453 / jnp.log(spot + 2.0)), 0.0)
    share = jnp.sum(share, axis=1, keepdims=True)
    ideal = jnp.sum(jnp.where(q_j == (case >> 2), share, 0.0), axis=0, keepdims=True)
    inverse = 1.0 / jnp.maximum(ideal, 1.0)

    mate = q_i == q_j
    earlier = iota((DOC, DOC), 1) < iota((DOC, DOC), 0)
    above = mate & ((s_j > s_i) | ((s_j == s_i) & earlier))
    above = jnp.where(above, 1.0, 0.0)
    rank_i = 1.0 + jnp.sum(above, axis=1, keepdims=True)
    rank_j = n_j - jnp.sum(above, axis=0, keepdims=True)
    disc_i = 0.6931471805599453 / jnp.log(1.0 + rank_i)
    disc_j = 0.6931471805599453 / jnp.log(1.0 + rank_j)
    step_gain = gain(l_i) - gain(l_j)
    odds = jnp.exp(s_i - s_j)
    miss = 1.0 / (1.0 + odds)
    swap = jnp.where(mate, jnp.abs(disc_i - disc_j) * w_i, 0.0) * miss
    push = swap * step_gain * jnp.where(step_gain > 0.0, 1.0, odds)
    bend = swap * jnp.abs(step_gain) * (odds * miss)
    scale = w_j * inverse
    grad = jnp.sum(push, axis=0, keepdims=True) * scale
    hess = jnp.sum(bend, axis=0, keepdims=True) * scale
    grad = grad.astype(BF16).astype(F32)
    hess = hess.astype(BF16).astype(F32)
    both = jnp.concatenate([grad, hess], axis=0)
    out_ref[...] = jnp.broadcast_to(both.reshape(1, 2, DOC), (ROWS, 2, DOC))


def sort_kernel(
    feat_ref, thr_ref, col_ref, parent_ref, bins_ref, owner_ref, slot_ref, out_ref, bits_ref, fold_ref, left_ref
):
    column = col_ref[0]
    parent = parent_ref[...]
    hot = jnp.where(iota((PARENTS, GROUP), 0) == parent, 1.0, 0.0)
    hot_b = hot.astype(BF16)
    earlier = earlier_matrix()
    carry = jnp.zeros((PARENTS, 1), F32)
    ranks = []
    for block in range(FEATS):
        part = hot[:, block * DOC : (block + 1) * DOC]
        before = nn(hot_b[:, block * DOC : (block + 1) * DOC], earlier) + carry
        ranks.append(jnp.sum(part * before, axis=0, keepdims=True))
        carry = carry + jnp.sum(part, axis=1, keepdims=True)
    target = parent.astype(F32) * float(CAP) + jnp.concatenate(ranks, axis=1)

    bits = jnp.zeros((1, GROUP), F32)
    for p in range(PARENTS):
        at = feat_ref[p] - column * SPAN
        here = jnp.where((at >= 0) & (at < SPAN), 1.0, 0.0)
        row = bins_ref[pl.ds(jnp.clip(at, 0, SPAN - 1), 1), :]
        right = (parent == p) & (row > thr_ref[p])
        bits = bits + jnp.where(right, here, 0.0)
    bits_ref[...] = bits

    own = (iota((1, GROUP), 1) >> 8) == column
    owner = jnp.concatenate([owner_ref[...].astype(F32) + 1.0] * FEATS, axis=1)
    slot = jnp.concatenate([slot_ref[...].astype(F32)] * FEATS, axis=1)
    left_ref[0:SPAN, :] = bins_ref[...].astype(F32).astype(BF16)
    extra = [jnp.where(own, owner, 0.0), jnp.where(own, slot, 0.0), bits, jnp.zeros_like(bits)]
    for q in range(4):
        left_ref[SPAN + q * 16 : SPAN + q * 16 + 16, :] = jnp.broadcast_to(extra[q], (16, GROUP)).astype(BF16)

    left = left_ref[...]
    line = iota((256, GROUP), 0).astype(F32)
    for pair in range(SLOTS // 256):
        pick = as_hot(line == (target - float(256 * pair)))
        got = nt(left, pick).astype(BF16)
        for half in range(2):
            t = pair * 2 + half
            for q in range(4):
                lanes = slice(q * 128, q * 128 + 128)
                cols = slice(half * 128, half * 128 + 128)
                fold_ref[t * 16 : t * 16 + 16, lanes] = got[q * 16 : q * 16 + 16, cols]
                fold_ref[320 + t * 16 : 336 + t * 16, lanes] = got[64 + q * 16 : 80 + q * 16, cols]
    folded = nn(fold_ref[...], swap_matrix())
    which = iota((16, 128), 0)
    for p in range(PARENTS):
        tail = jnp.zeros((16, 128), F32)
        for g in range(5):
            t, a = divmod(p * 5 + g, 4)
            block = folded[t * 16 : t * 16 + 16, a * 128 : a * 128 + 128].astype(BF16)
            out_ref[p, g * 16 : g * 16 + 16, :] = block
            tail = jnp.where(which == g, folded[320 + t * 16 : 336 + t * 16, a * 128 : a * 128 + 128], tail)
        out_ref[p, 80:88, :] = tail[0:8].astype(BF16)


def open_kernel(in_ref, bins_ref, extra_ref):
    swap = swap_matrix()
    for r in range(PEERS // 4):
        four = jnp.concatenate([in_ref[4 * r + a] for a in range(4)], axis=1)
        flat = nn(four, swap)
        for g in range(5):
            t = r * 5 + g
            for q in range(4):
                bins_ref[q * 16 : q * 16 + 16, t * 128 : t * 128 + 128] = flat[
                    g * 16 : g * 16 + 16, q * 128 : q * 128 + 128
                ].astype(BF16)
        for q in range(3):
            extra_ref[q, r] = flat[80:88, q * 128 : q * 128 + 128]


def pick_kernel(grads_ref, extra_ref, bits_ref, out_ref, all_ref):
    turned = jnp.concatenate([jnp.transpose(grads_ref[:, k, :]) for k in range(2)], axis=0)
    turned = turned.astype(BF16)
    owner_line = (iota((ROWS, 128), 0) + 1).astype(F32)
    slot_line = iota((DOC, 128), 0).astype(F32)
    for t in range(TILES):
        r, g = divmod(t, 5)
        owner = extra_ref[0, r, g : g + 1, :]
        slot = extra_ref[1, r, g : g + 1, :]
        from_owner = nn(turned, as_hot(owner_line == owner))
        hit = slot_line == slot
        for k in range(2):
            mine = jnp.where(hit, from_owner[k * DOC : k * DOC + DOC], 0.0)
            all_ref[k * TILES + t : k * TILES + t + 1, :] = jnp.sum(mine, axis=0, keepdims=True)
        all_ref[2 * TILES + t : 2 * TILES + t + 1, :] = extra_ref[2, r, g : g + 1, :]
    all_ref[62:64, :] = jnp.zeros((2, 128), F32)
    for c in range(FEATS):
        all_ref[60:62, :] = bits_ref[2 * c : 2 * c + 2, :]
        out_ref[c] = all_ref[...].astype(BF16)


def histogram_kernel(col_ref, shares_ref, bins_ref, parent_ref, out_ref, node_ref, sums_ref, vals_ref):
    sums = shares_ref[0].astype(F32)
    for c in range(1, FEATS):
        sums = sums + shares_ref[c].astype(F32)
    sums_ref[...] = sums
    node_ref[...] = 2 * parent_ref[pl.ds(2 * col_ref[0], 2), :] + sums_ref[60:62, :].astype(I32)

    child = (iota((16, 128), 0) >> 3).astype(F32)
    for t in range(TILES):
        bit = sums_ref[2 * TILES + t : 2 * TILES + t + 1, :]
        for k in range(2):
            value = sums_ref[k * TILES + t : k * TILES + t + 1, :]
            vals_ref[k * 16 : k * 16 + 16, t * 128 : t * 128 + 128] = jnp.where(
                child == bit, value, 0.0
            ).astype(BF16)

    vals = [vals_ref[0:16, :], vals_ref[16:32, :]]
    zero = jnp.zeros((16, TAKEN), BF16)
    one = jnp.ones((16, TAKEN), BF16)
    odd = iota((16, TAKEN), 0) >> 3
    row = iota((256, 256), 0)
    lane = iota((256, 256), 1)
    own = (row & 7) == (lane & 7)
    fold = as_hot((row >> 3) == (lane & 31))
    block = iota((32, 256), 1) >> 5
    for g in range(SPAN // 8):
        bins = bins_ref[g // 2 * 16 : g // 2 * 16 + 16, :].astype(F32)
        bins = bins[g % 2 * 8 : g % 2 * 8 + 8, :]
        high = jnp.floor(bins * (1.0 / 32.0))
        low = bins - high * 32.0
        high = jnp.concatenate([high, high], axis=0).astype(BF16)
        low = (jnp.concatenate([low, low], axis=0) - odd.astype(F32)).astype(BF16)
        tall = []
        for h in range(8):
            hit = high == jnp.array(h, BF16)
            tall += [jnp.where(hit, v, zero) for v in vals]
        flat = [jnp.where(low == jnp.array(2 * l, BF16), one, zero) for l in range(16)]
        acc = nt(jnp.concatenate(tall, axis=0), jnp.concatenate(flat, axis=0))
        parts = three_parts(jnp.where(own, acc, 0.0))
        wide = sum([nn(part.astype(BF16), fold) for part in parts])
        total = jnp.zeros((32, 256), F32)
        for h in range(8):
            total = jnp.where(block == h, wide[h * 32 : h * 32 + 32, :], total)
        for k in range(4):
            out_ref[k, g * 8 : g * 8 + 8, :] = total[k * 8 : k * 8 + 8, :]


SMEM = pl.BlockSpec(memory_space=pltpu.SMEM)
VMEM = pl.BlockSpec(memory_space=pltpu.VMEM)


def call(kernel, ins, outs, scratch=(), **more):
    return pl.pallas_call(
        kernel,
        out_shape=[jax.ShapeDtypeStruct(s, d) for s, d in outs],
        in_specs=list(ins),
        out_specs=[VMEM] * len(outs),
        scratch_shapes=list(scratch),
        **more,
    )


def exchange(x, **more):
    return lax.all_to_all(x, "rows", split_axis=0, concat_axis=0, tiled=True, **more)


def local(
    scores, weights, labels, owner_row, owner_slot, query_len, bin_index, parent, split_feat, split_thr
):
    column = lax.axis_index("feat").astype(I32).reshape(1)
    classes = [[32 * h + 2 * i + k for i in range(PEERS)] for h in range(2) for k in range(2)]
    quads = [[2 * p, 2 * p + 1, 32 + 2 * p, 33 + 2 * p] for p in range(PARENTS)]

    def line(x):
        return x.reshape(1, DOC)

    (outbound,) = call(send_kernel, [VMEM] * 5, [((ROWS, 1, 128), F32)])(
        line(scores), line(weights), line(labels), line(owner_row), line(owner_slot)
    )
    inbound = exchange(outbound)
    sorted_docs, bits = call(
        sort_kernel,
        [SMEM] * 3 + [VMEM] * 4,
        [((PEERS, CHUNK, 128), BF16), ((1, GROUP), F32)],
        [pltpu.VMEM((640, 512), BF16), pltpu.VMEM((128, GROUP), BF16)],
    )(
        split_feat,
        split_thr,
        column,
        parent.reshape(1, GROUP),
        bin_index,
        line(owner_row),
        line(owner_slot),
    )
    taken = exchange(sorted_docs, axis_index_groups=classes)
    (spread,) = call(owner_kernel, [SMEM, VMEM], [((ROWS, 2, DOC), F32)])(query_len, inbound)
    grads = exchange(spread)
    bins, extra = call(
        open_kernel, [VMEM], [((SPAN, TAKEN), BF16), ((3, PEERS // 4, 8, 128), F32)]
    )(taken)
    (share,) = call(
        pick_kernel, [VMEM] * 3, [((FEATS, SHARE, 128), BF16)], [pltpu.VMEM((SHARE, 128), F32)]
    )(grads, extra, bits.reshape(16, 128))
    shares = lax.all_to_all(share, "feat", split_axis=0, concat_axis=0, tiled=True)
    rows, new_node = call(
        histogram_kernel,
        [SMEM] + [VMEM] * 3,
        [((4, SPAN, BINS), F32), ((2, 128), I32)],
        [pltpu.VMEM((SHARE, 128), F32), pltpu.VMEM((32, TAKEN), BF16)],
    )(column, shares, bins, parent.reshape(16, 128))
    came = exchange(rows, axis_index_groups=quads)
    return (jnp.sum(came, axis=0, keepdims=True), new_node.reshape(DOC))


def solution(mesh):
    docs = P(("rows", "feat"))
    placed = (docs,) * 5 + (P(("rows", "feat"), None), P("feat", "rows"), P("rows"), P(), P())
    return jax.shard_map(
        local,
        mesh=mesh,
        in_specs=placed,
        out_specs=(P("rows", "feat", None), docs),
        check_vma=False,
    )
```

```python
import functools

import jax
import jax.numpy as jnp
from jax import lax
from jax.experimental import pallas as pl
from jax.experimental.pallas import tpu as pltpu
from jax.sharding import PartitionSpec as P

BINS = 256
NODES = 32
QMAX = 128
PARENTS = 16
ROWS = 64
FEATS = 8
DOC = 256
GROUP = FEATS * DOC
SPAN = 64
CAP = 160
SLOTS = PARENTS * CAP
POS = 8
PEERS = 16
TAKEN = PEERS * CAP
TILES = TAKEN // 128
CHUNK = 88
SHARE = 64

F32 = jnp.float32
BF16 = jnp.bfloat16
I32 = jnp.int32


def iota(shape, dim):
    return lax.broadcasted_iota(I32, shape, dim)


def nt(a, b):
    return lax.dot_general(a, b, (((1,), (1,)), ((), ())), preferred_element_type=F32)


def nn(a, b):
    return jnp.dot(a, b, preferred_element_type=F32)


def as_hot(mask):
    return jnp.where(mask, 1.0, 0.0).astype(BF16)


def three_parts(x):
    top = x.astype(BF16).astype(F32)
    rest = x - top
    middle = rest.astype(BF16).astype(F32)
    return top, middle, rest - middle


def swap_matrix():
    row = iota((512, 1), 0)
    goal = ((row >> 5) & 3) * 128 + (row >> 7) * 32 + (row & 31)
    return as_hot(goal == iota((512, 512), 1))


def earlier_matrix():
    return as_hot(iota((DOC, DOC), 0) < iota((DOC, DOC), 1))


def stack_rows(rows, height, width):
    place = iota((height, width), 0)
    out = jnp.zeros((height, width), F32)
    for at, row in enumerate(rows):
        out = jnp.where(place == at, row, out)
    return out


def send_kernel(score_ref, weight_ref, label_ref, owner_ref, slot_ref, out_ref):
    owner = owner_ref[...]
    hot = jnp.where(iota((ROWS, DOC), 0) == owner, 1.0, 0.0)
    before = nn(hot.astype(BF16), earlier_matrix())
    place = jnp.sum(hot * before, axis=0, keepdims=True)
    rows = [
        *three_parts(score_ref[...]),
        *three_parts(weight_ref[...]),
        slot_ref[...].astype(F32) + 1.0,
        label_ref[...].astype(F32),
    ]
    values = stack_rows(rows, 16, DOC)
    tiled = jnp.concatenate([values] * POS, axis=0)
    group = iota((16 * POS, DOC), 0) >> 4
    total = jnp.zeros((ROWS, 128), F32)
    for pos in range(POS):
        here = jnp.where(place == float(pos), hot, 0.0).astype(BF16)
        total += nt(here, jnp.where(group == pos, tiled, 0.0).astype(BF16))
    out_ref[:, 0, :] = total


def owner_kernel(len_ref, in_ref, out_ref):
    data = in_ref[:, 0, :]
    turned = jnp.transpose(data).astype(BF16)
    lane = iota((ROWS, DOC), 1).astype(F32) + 1.0
    table = jnp.zeros((16, DOC), F32)
    for pos in range(POS):
        hot = as_hot(data[:, pos * 16 + 6 : pos * 16 + 7] == lane)
        table += nn(turned[pos * 16 : pos * 16 + 16, :], hot)
    same = as_hot(iota((DOC, DOC), 0) == iota((DOC, DOC), 1))
    upright = nt(same, table.astype(BF16))
    s_j = table[0:1] + table[1:2] + table[2:3]
    w_j = table[3:4] + table[4:5] + table[5:6]
    l_j = table[7:8]
    s_i = upright[:, 0:1] + upright[:, 1:2] + upright[:, 2:3]
    w_i = upright[:, 3:4] + upright[:, 4:5] + upright[:, 5:6]
    l_i = upright[:, 7:8]

    ends = []
    total = 0
    for q in range(3):
        total = total + len_ref[0, q]
        ends.append(total)

    def query_of(at):
        return sum([(at >= end).astype(I32) for end in ends])

    def gain(label):
        return sum([jnp.where(label >= float(l), 2.0 ** (l - 1), 0.0) for l in range(1, 5)])

    row_at = iota((1, DOC), 1)
    q_j = query_of(row_at)
    q_i = query_of(iota((DOC, 1), 0))
    n_j = jnp.zeros((1, DOC), F32)
    for q in range(4):
        n_j = jnp.where(q_j == q, len_ref[0, q].astype(F32), n_j)

    case = iota((16, DOC), 0)
    level = ((case & 3) + 1).astype(F32)
    reaches = (q_j == (case >> 2)) & (l_j >= level)
    count = jnp.sum(jnp.where(reaches, 1.0, 0.0), axis=1, keepdims=True)
    spot = iota((16, QMAX), 1).astype(F32)
    step = jnp.left_shift(1, iota((16, QMAX), 0) & 3).astype(F32)
    share = jnp.where(spot < count, step * (0.6931471805599453 / jnp.log(spot + 2.0)), 0.0)
    share = jnp.sum(share, axis=1, keepdims=True)
    ideal = jnp.sum(jnp.where(q_j == (case >> 2), share, 0.0), axis=0, keepdims=True)
    inverse = 1.0 / jnp.maximum(ideal, 1.0)

    mate = q_i == q_j
    earlier = iota((DOC, DOC), 1) < iota((DOC, DOC), 0)
    above = mate & ((s_j > s_i) | ((s_j == s_i) & earlier))
    above = jnp.where(above, 1.0, 0.0)
    rank_i = 1.0 + jnp.sum(above, axis=1, keepdims=True)
    rank_j = n_j - jnp.sum(above, axis=0, keepdims=True)
    disc_i = 0.6931471805599453 / jnp.log(1.0 + rank_i)
    disc_j = 0.6931471805599453 / jnp.log(1.0 + rank_j)
    step_gain = gain(l_i) - gain(l_j)
    odds = jnp.exp(s_i - s_j)
    miss = 1.0 / (1.0 + odds)
    swap = jnp.where(mate, jnp.abs(disc_i - disc_j) * w_i, 0.0) * miss
    push = swap * step_gain * jnp.where(step_gain > 0.0, 1.0, odds)
    bend = swap * jnp.abs(step_gain) * (odds * miss)
    scale = w_j * inverse
    grad = jnp.sum(push, axis=0, keepdims=True) * scale
    hess = jnp.sum(bend, axis=0, keepdims=True) * scale
    both = jnp.concatenate([grad, hess], axis=0).astype(BF16)
    for r in range(ROWS):
        out_ref[r] = both


def sort_kernel(
    feat_ref, thr_ref, col_ref, parent_ref, bins_ref, owner_ref, slot_ref, out_ref, bits_ref, fold_ref, left_ref, tail_ref
):
    column = col_ref[0]
    parent = parent_ref[...]
    hot = jnp.where(iota((PARENTS, GROUP), 0) == parent, 1.0, 0.0)
    hot_b = hot.astype(BF16)
    earlier = earlier_matrix()
    carry = jnp.zeros((PARENTS, 1), F32)
    ranks = []
    for block in range(FEATS):
        part = hot[:, block * DOC : (block + 1) * DOC]
        before = nn(hot_b[:, block * DOC : (block + 1) * DOC], earlier) + carry
        ranks.append(jnp.sum(part * before, axis=0, keepdims=True))
        carry = carry + jnp.sum(part, axis=1, keepdims=True)
    rank = jnp.concatenate(ranks, axis=1)

    bits = jnp.zeros((1, GROUP), F32)
    for p in range(PARENTS):
        at = feat_ref[p] - column * SPAN
        here = jnp.where((at >= 0) & (at < SPAN), 1.0, 0.0)
        row = bins_ref[pl.ds(jnp.clip(at, 0, SPAN - 1), 1), :]
        right = (parent == p) & (row > thr_ref[p])
        bits = bits + jnp.where(right, here, 0.0)
    bits_ref[...] = bits

    own = (iota((1, GROUP), 1) >> 8) == column
    owner = jnp.concatenate([owner_ref[...].astype(F32) + 1.0] * FEATS, axis=1)
    slot = jnp.concatenate([slot_ref[...].astype(F32)] * FEATS, axis=1)
    left_ref[0:SPAN, :] = bins_ref[...].astype(F32).astype(BF16)
    extra = [jnp.where(own, owner, 0.0), jnp.where(own, slot, 0.0), bits]
    left_ref[SPAN : SPAN + 16, :] = stack_rows(extra, 16, GROUP).astype(BF16)

    left = left_ref[...]
    pick = as_hot(iota((CAP, GROUP), 0).astype(F32) == rank)
    each = jnp.concatenate([left * hot_b[p : p + 1, :] for p in range(PARENTS)], axis=0)
    gathered = nt(each, pick)
    for p in range(PARENTS):
        got = gathered[p * 80 : p * 80 + 80, :]
        low = got.astype(BF16)
        for q in range(4):
            lanes = slice(q * 128, q * 128 + 128)
            rows = slice(q * 16, q * 16 + 16)
            fold_ref[p * 16 : p * 16 + 16, lanes] = low[rows, 0:128]
            ext = jnp.broadcast_to(got[SPAN + q : SPAN + q + 1, :], (16, CAP)).astype(BF16)
            fold_ref[256 + p * 16 : 272 + p * 16, lanes] = ext[:, 0:128]
            tail_ref[p * 16 : p * 16 + 16, q * 32 : q * 32 + 32] = low[rows, 128:160]
            tail_ref[256 + p * 16 : 272 + p * 16, q * 32 : q * 32 + 32] = ext[:, 128:160]
    folded = nn(fold_ref[...], swap_matrix())
    which = iota((16, 128), 0)
    for p in range(PARENTS):
        for g in range(4):
            out_ref[p, g * 16 : g * 16 + 16, :] = folded[
                p * 16 : p * 16 + 16, g * 128 : g * 128 + 128
            ].astype(BF16)
        out_ref[p, 64:80, :] = tail_ref[p * 16 : p * 16 + 16, :]
        last = tail_ref[256 + p * 16 : 272 + p * 16, :].astype(F32)
        for g in range(4):
            last = jnp.where(which == g, folded[256 + p * 16 : 272 + p * 16, g * 128 : g * 128 + 128], last)
        out_ref[p, 80:88, :] = last[0:8].astype(BF16)


def open_kernel(in_ref, bins_ref, extra_ref):
    swap = swap_matrix()
    for r in range(PEERS // 4):
        four = jnp.concatenate([in_ref[4 * r + a] for a in range(4)], axis=1)
        flat = nn(four, swap)
        for g in range(5):
            t = r * 5 + g
            for q in range(4):
                bins_ref[q * 16 : q * 16 + 16, t * 128 : t * 128 + 128] = flat[
                    g * 16 : g * 16 + 16, q * 128 : q * 128 + 128
                ].astype(BF16)
        for q in range(3):
            extra_ref[q, r] = flat[80:88, q * 128 : q * 128 + 128]


def pick_kernel(grads_ref, extra_ref, bits_ref, out_ref, all_ref):
    turned = jnp.concatenate([jnp.transpose(grads_ref[:, k, :].astype(F32)) for k in range(2)], axis=0)
    turned = turned.astype(BF16)
    owner_line = (iota((ROWS, 128), 0) + 1).astype(F32)
    slot_line = iota((DOC, 128), 0).astype(F32)
    for t in range(TILES):
        r, g = divmod(t, 5)
        owner = extra_ref[0, r, g : g + 1, :]
        slot = extra_ref[1, r, g : g + 1, :]
        from_owner = nn(turned, as_hot(owner_line == owner))
        hit = slot_line == slot
        for k in range(2):
            mine = jnp.where(hit, from_owner[k * DOC : k * DOC + DOC], 0.0)
            all_ref[k * TILES + t : k * TILES + t + 1, :] = jnp.sum(mine, axis=0, keepdims=True)
        all_ref[2 * TILES + t : 2 * TILES + t + 1, :] = extra_ref[2, r, g : g + 1, :]
    all_ref[62:64, :] = jnp.zeros((2, 128), F32)
    for c in range(FEATS):
        all_ref[60:62, :] = bits_ref[2 * c : 2 * c + 2, :]
        out_ref[c] = all_ref[...].astype(BF16)


def histogram_kernel(col_ref, shares_ref, bins_ref, parent_ref, out_ref, node_ref, sums_ref, vals_ref, acc_ref):
    sums = shares_ref[0].astype(F32)
    for c in range(1, FEATS):
        sums = sums + shares_ref[c].astype(F32)
    sums_ref[...] = sums
    node_ref[...] = 2 * parent_ref[pl.ds(2 * col_ref[0], 2), :] + sums_ref[60:62, :].astype(I32)

    child = (iota((16, 128), 0) >> 3).astype(F32)
    for t in range(TILES):
        bit = sums_ref[2 * TILES + t : 2 * TILES + t + 1, :]
        for k in range(2):
            value = sums_ref[k * TILES + t : k * TILES + t + 1, :]
            vals_ref[k * 16 : k * 16 + 16, t * 128 : t * 128 + 128] = jnp.where(
                child == bit, value, 0.0
            ).astype(BF16)

    vals = [vals_ref[0:16, :], vals_ref[16:32, :]]
    zero = jnp.zeros((16, TAKEN), BF16)
    one = jnp.ones((16, TAKEN), BF16)
    odd = iota((16, TAKEN), 0) >> 3
    row = iota((256, 256), 0)
    lane = iota((256, 256), 1)
    own = (row & 7) == (lane & 7)
    fold = as_hot((row >> 3) == (lane & 31))
    block = iota((32, 256), 1) >> 5
    for g in range(SPAN // 8):
        bins = bins_ref[g // 2 * 16 : g // 2 * 16 + 16, :].astype(F32)
        bins = bins[g % 2 * 8 : g % 2 * 8 + 8, :]
        high = jnp.floor(bins * (1.0 / 32.0))
        low = bins - high * 32.0
        high = jnp.concatenate([high, high], axis=0).astype(BF16)
        low = (jnp.concatenate([low, low], axis=0) - odd.astype(F32)).astype(BF16)
        tall = []
        for h in range(8):
            hit = high == jnp.array(h, BF16)
            tall += [jnp.where(hit, v, zero) for v in vals]
        flat = [jnp.where(low == jnp.array(2 * l, BF16), one, zero) for l in range(16)]
        acc_ref[g * 256 : g * 256 + 256, :] = nt(jnp.concatenate(tall, axis=0), jnp.concatenate(flat, axis=0))
    two = jnp.concatenate([fold, fold], axis=0)
    for g in range(SPAN // 8):
        acc = jnp.where(own, acc_ref[g * 256 : g * 256 + 256, :], 0.0)
        top = acc.astype(BF16)
        rest = (acc - top.astype(F32)).astype(BF16)
        wide = nn(jnp.concatenate([top, rest], axis=1), two)
        total = jnp.zeros((32, 256), F32)
        for h in range(8):
            total = jnp.where(block == h, wide[h * 32 : h * 32 + 32, :], total)
        for k in range(4):
            out_ref[k, g * 8 : g * 8 + 8, :] = total[k * 8 : k * 8 + 8, :]


SMEM = pl.BlockSpec(memory_space=pltpu.SMEM)
VMEM = pl.BlockSpec(memory_space=pltpu.VMEM)


def call(kernel, ins, outs, scratch=(), **more):
    return pl.pallas_call(
        kernel,
        out_shape=[pltpu.VMEM(s, d) for s, d in outs],
        in_specs=list(ins),
        out_specs=[VMEM] * len(outs),
        scratch_shapes=list(scratch),
        **more,
    )


def near(x):
    return pltpu.with_memory_space_constraint(x, pltpu.VMEM)


def exchange(x, **more):
    return lax.all_to_all(x, "rows", split_axis=0, concat_axis=0, tiled=True, **more)


def local(
    scores, weights, labels, owner_row, owner_slot, query_len, bin_index, parent, split_feat, split_thr
):
    column = lax.axis_index("feat").astype(I32).reshape(1)
    classes = [[32 * h + 2 * i + k for i in range(PEERS)] for h in range(2) for k in range(2)]
    quads = [[2 * p, 2 * p + 1, 32 + 2 * p, 33 + 2 * p] for p in range(PARENTS)]

    def line(x):
        return x.reshape(1, DOC)

    (outbound,) = call(send_kernel, [VMEM] * 5, [((ROWS, 1, 128), F32)])(
        line(scores), line(weights), line(labels), line(owner_row), line(owner_slot)
    )
    inbound = exchange(outbound)
    sorted_docs, bits = call(
        sort_kernel,
        [SMEM] * 3 + [VMEM] * 4,
        [((PEERS, CHUNK, 128), BF16), ((1, GROUP), F32)],
        [pltpu.VMEM((512, 512), BF16), pltpu.VMEM((80, GROUP), BF16), pltpu.VMEM((512, 128), BF16)],
    )(
        split_feat,
        split_thr,
        column,
        parent.reshape(1, GROUP),
        bin_index,
        line(owner_row),
        line(owner_slot),
    )
    taken = exchange(sorted_docs, axis_index_groups=classes)
    (spread,) = call(owner_kernel, [SMEM, VMEM], [((ROWS, 2, DOC), BF16)])(query_len, near(inbound))
    grads = exchange(spread)
    bins, extra = call(
        open_kernel, [VMEM], [((SPAN, TAKEN), BF16), ((3, PEERS // 4, 8, 128), F32)]
    )(near(taken))
    (share,) = call(
        pick_kernel, [VMEM] * 3, [((FEATS, SHARE, 128), BF16)], [pltpu.VMEM((SHARE, 128), F32)]
    )(near(grads), near(extra), near(bits.reshape(16, 128)))
    shares = lax.all_to_all(share, "feat", split_axis=0, concat_axis=0, tiled=True)
    rows, new_node = call(
        histogram_kernel,
        [SMEM] + [VMEM] * 3,
        [((4, SPAN, BINS), F32), ((2, 128), I32)],
        [
            pltpu.VMEM((SHARE, 128), F32),
            pltpu.VMEM((32, TAKEN), BF16),
            pltpu.VMEM((SPAN // 8 * 256, 256), F32),
        ],
    )(column, near(shares), near(bins), parent.reshape(16, 128))
    came = exchange(rows, axis_index_groups=quads)
    return (jnp.sum(came, axis=0, keepdims=True), new_node.reshape(DOC))


def solution(mesh):
    docs = P(("rows", "feat"))
    placed = (docs,) * 5 + (P(("rows", "feat"), None), P("feat", "rows"), P("rows"), P(), P())
    return jax.shard_map(
        local,
        mesh=mesh,
        in_specs=placed,
        out_specs=(P("rows", "feat", None), docs),
        check_vma=False,
    )
```

```python
import functools

import jax
import jax.numpy as jnp
from jax import lax
from jax.experimental import pallas as pl
from jax.experimental.pallas import tpu as pltpu
from jax.sharding import PartitionSpec as P

BINS = 256
NODES = 32
QMAX = 128
PARENTS = 16
ROWS = 64
FEATS = 8
DOC = 256
GROUP = FEATS * DOC
SPAN = 64
CAP = 160
SLOTS = PARENTS * CAP
POS = 8
PEERS = 16
TAKEN = PEERS * CAP
TILES = TAKEN // 128
CHUNK = 88
SHARE = 64

SCORE_UP = 2.0**40

F32 = jnp.float32
BF16 = jnp.bfloat16
I32 = jnp.int32


def iota(shape, dim):
    return lax.broadcasted_iota(I32, shape, dim)


def nt(a, b):
    return lax.dot_general(a, b, (((1,), (1,)), ((), ())), preferred_element_type=F32)


def nn(a, b):
    return jnp.dot(a, b, preferred_element_type=F32)


def as_hot(mask):
    return jnp.where(mask, 1.0, 0.0).astype(BF16)


def three_parts(x):
    top = x.astype(BF16).astype(F32)
    rest = x - top
    middle = rest.astype(BF16).astype(F32)
    return top, middle, rest - middle


def swap_matrix():
    row = iota((512, 1), 0)
    goal = ((row >> 5) & 3) * 128 + (row >> 7) * 32 + (row & 31)
    return as_hot(goal == iota((512, 512), 1))


def earlier_matrix():
    return as_hot(iota((DOC, DOC), 0) < iota((DOC, DOC), 1))


def stack_rows(rows, height, width):
    place = iota((height, width), 0)
    out = jnp.zeros((height, width), F32)
    for at, row in enumerate(rows):
        out = jnp.where(place == at, row, out)
    return out


def send_kernel(score_ref, weight_ref, label_ref, owner_ref, slot_ref, out_ref):
    owner = owner_ref[...]
    hot = jnp.where(iota((ROWS, DOC), 0) == owner, 1.0, 0.0)
    before = nn(hot.astype(BF16), earlier_matrix())
    place = jnp.sum(hot * before, axis=0, keepdims=True)
    rows = [
        *three_parts(score_ref[...] * SCORE_UP),
        *three_parts(weight_ref[...]),
        slot_ref[...].astype(F32) + 1.0,
        label_ref[...].astype(F32),
    ]
    values = stack_rows(rows, 16, DOC)
    tiled = jnp.concatenate([values] * POS, axis=0)
    group = iota((16 * POS, DOC), 0) >> 4
    total = jnp.zeros((ROWS, 128), F32)
    for pos in range(POS):
        here = jnp.where(place == float(pos), hot, 0.0).astype(BF16)
        total += nt(here, jnp.where(group == pos, tiled, 0.0).astype(BF16))
    out_ref[:, 0, :] = total


def owner_kernel(len_ref, in_ref, out_ref):
    data = in_ref[:, 0, :]
    turned = jnp.transpose(data).astype(BF16)
    lane = iota((ROWS, DOC), 1).astype(F32) + 1.0
    table = jnp.zeros((16, DOC), F32)
    for pos in range(POS):
        hot = as_hot(data[:, pos * 16 + 6 : pos * 16 + 7] == lane)
        table += nn(turned[pos * 16 : pos * 16 + 16, :], hot)
    same = as_hot(iota((DOC, DOC), 0) == iota((DOC, DOC), 1))
    upright = nt(same, table.astype(BF16))
    s_j = (table[0:1] + table[1:2] + table[2:3]) * (1.0 / SCORE_UP)
    w_j = table[3:4] + table[4:5] + table[5:6]
    l_j = table[7:8]
    s_i = (upright[:, 0:1] + upright[:, 1:2] + upright[:, 2:3]) * (1.0 / SCORE_UP)
    w_i = upright[:, 3:4] + upright[:, 4:5] + upright[:, 5:6]
    l_i = upright[:, 7:8]

    ends = []
    total = 0
    for q in range(3):
        total = total + len_ref[0, q]
        ends.append(total)

    def query_of(at):
        return sum([(at >= end).astype(I32) for end in ends])

    def gain(label):
        return sum([jnp.where(label >= float(l), 2.0 ** (l - 1), 0.0) for l in range(1, 5)])

    row_at = iota((1, DOC), 1)
    q_j = query_of(row_at)
    q_i = query_of(iota((DOC, 1), 0))
    n_j = jnp.zeros((1, DOC), F32)
    for q in range(4):
        n_j = jnp.where(q_j == q, len_ref[0, q].astype(F32), n_j)

    case = iota((16, DOC), 0)
    level = ((case & 3) + 1).astype(F32)
    reaches = (q_j == (case >> 2)) & (l_j >= level)
    count = jnp.sum(jnp.where(reaches, 1.0, 0.0), axis=1, keepdims=True)
    spot = iota((16, QMAX), 1).astype(F32)
    step = jnp.left_shift(1, iota((16, QMAX), 0) & 3).astype(F32)
    share = jnp.where(spot < count, step * (0.6931471805599453 / jnp.log(spot + 2.0)), 0.0)
    share = jnp.sum(share, axis=1, keepdims=True)
    ideal = jnp.sum(jnp.where(q_j == (case >> 2), share, 0.0), axis=0, keepdims=True)
    inverse = 1.0 / jnp.maximum(ideal, 1.0)

    mate = q_i == q_j
    earlier = iota((DOC, DOC), 1) < iota((DOC, DOC), 0)
    above = mate & ((s_j > s_i) | ((s_j == s_i) & earlier))
    above = jnp.where(above, 1.0, 0.0)
    rank_i = 1.0 + jnp.sum(above, axis=1, keepdims=True)
    rank_j = n_j - jnp.sum(above, axis=0, keepdims=True)
    disc_i = 0.6931471805599453 / jnp.log(1.0 + rank_i)
    disc_j = 0.6931471805599453 / jnp.log(1.0 + rank_j)
    step_gain = gain(l_i) - gain(l_j)
    odds = jnp.exp(s_i - s_j)
    miss = 1.0 / (1.0 + odds)
    swap = jnp.where(mate, jnp.abs(disc_i - disc_j) * w_i, 0.0) * miss
    push = swap * step_gain * jnp.where(step_gain > 0.0, 1.0, odds)
    bend = swap * jnp.abs(step_gain) * (odds * miss)
    scale = w_j * inverse
    grad = jnp.sum(push, axis=0, keepdims=True) * scale
    hess = jnp.sum(bend, axis=0, keepdims=True) * scale
    both = jnp.concatenate([grad, hess], axis=0).astype(BF16)
    for r in range(ROWS):
        out_ref[r] = both


def sort_kernel(
    feat_ref, thr_ref, col_ref, parent_ref, bins_ref, owner_ref, slot_ref, out_ref, bits_ref, fold_ref, left_ref, tail_ref
):
    column = col_ref[0]
    parent = parent_ref[...]
    hot = jnp.where(iota((PARENTS, GROUP), 0) == parent, 1.0, 0.0)
    hot_b = hot.astype(BF16)
    earlier = earlier_matrix()
    carry = jnp.zeros((PARENTS, 1), F32)
    ranks = []
    for block in range(FEATS):
        part = hot[:, block * DOC : (block + 1) * DOC]
        before = nn(hot_b[:, block * DOC : (block + 1) * DOC], earlier) + carry
        ranks.append(jnp.sum(part * before, axis=0, keepdims=True))
        carry = carry + jnp.sum(part, axis=1, keepdims=True)
    rank = jnp.concatenate(ranks, axis=1)

    bits = jnp.zeros((1, GROUP), F32)
    for p in range(PARENTS):
        at = feat_ref[p] - column * SPAN
        here = jnp.where((at >= 0) & (at < SPAN), 1.0, 0.0)
        row = bins_ref[pl.ds(jnp.clip(at, 0, SPAN - 1), 1), :]
        right = (parent == p) & (row > thr_ref[p])
        bits = bits + jnp.where(right, here, 0.0)
    bits_ref[...] = bits

    own = (iota((1, GROUP), 1) >> 8) == column
    owner = jnp.concatenate([owner_ref[...].astype(F32) + 1.0] * FEATS, axis=1)
    slot = jnp.concatenate([slot_ref[...].astype(F32)] * FEATS, axis=1)
    left_ref[0:SPAN, :] = bins_ref[...].astype(F32).astype(BF16)
    extra = [jnp.where(own, owner, 0.0), jnp.where(own, slot, 0.0), bits]
    left_ref[SPAN : SPAN + 16, :] = stack_rows(extra, 16, GROUP).astype(BF16)

    left = left_ref[...]
    pick = as_hot(iota((CAP, GROUP), 0).astype(F32) == rank)
    each = jnp.concatenate([left * hot_b[p : p + 1, :] for p in range(PARENTS)], axis=0)
    gathered = nt(each, pick)
    for p in range(PARENTS):
        got = gathered[p * 80 : p * 80 + 80, :]
        low = got.astype(BF16)
        for q in range(4):
            lanes = slice(q * 128, q * 128 + 128)
            rows = slice(q * 16, q * 16 + 16)
            fold_ref[p * 16 : p * 16 + 16, lanes] = low[rows, 0:128]
            ext = jnp.broadcast_to(got[SPAN + q : SPAN + q + 1, :], (16, CAP)).astype(BF16)
            fold_ref[256 + p * 16 : 272 + p * 16, lanes] = ext[:, 0:128]
            tail_ref[p * 16 : p * 16 + 16, q * 32 : q * 32 + 32] = low[rows, 128:160]
            tail_ref[256 + p * 16 : 272 + p * 16, q * 32 : q * 32 + 32] = ext[:, 128:160]
    folded = nn(fold_ref[...], swap_matrix())
    which = iota((16, 128), 0)
    for p in range(PARENTS):
        for g in range(4):
            out_ref[p, g * 16 : g * 16 + 16, :] = folded[
                p * 16 : p * 16 + 16, g * 128 : g * 128 + 128
            ].astype(BF16)
        out_ref[p, 64:80, :] = tail_ref[p * 16 : p * 16 + 16, :]
        last = tail_ref[256 + p * 16 : 272 + p * 16, :].astype(F32)
        for g in range(4):
            last = jnp.where(which == g, folded[256 + p * 16 : 272 + p * 16, g * 128 : g * 128 + 128], last)
        out_ref[p, 80:88, :] = last[0:8].astype(BF16)


def open_kernel(in_ref, bins_ref, extra_ref):
    swap = swap_matrix()
    for r in range(PEERS // 4):
        four = jnp.concatenate([in_ref[4 * r + a] for a in range(4)], axis=1)
        flat = nn(four, swap)
        for g in range(5):
            t = r * 5 + g
            for q in range(4):
                bins_ref[q * 16 : q * 16 + 16, t * 128 : t * 128 + 128] = flat[
                    g * 16 : g * 16 + 16, q * 128 : q * 128 + 128
                ].astype(BF16)
        for q in range(3):
            extra_ref[q, r] = flat[80:88, q * 128 : q * 128 + 128]


def pick_kernel(grads_ref, extra_ref, bits_ref, out_ref, all_ref):
    turned = jnp.concatenate([jnp.transpose(grads_ref[:, k, :].astype(F32)) for k in range(2)], axis=0)
    turned = turned.astype(BF16)
    owner_line = (iota((ROWS, 128), 0) + 1).astype(F32)
    slot_line = iota((DOC, 128), 0).astype(F32)
    for t in range(TILES):
        r, g = divmod(t, 5)
        owner = extra_ref[0, r, g : g + 1, :]
        slot = extra_ref[1, r, g : g + 1, :]
        from_owner = nn(turned, as_hot(owner_line == owner))
        hit = slot_line == slot
        for k in range(2):
            mine = jnp.where(hit, from_owner[k * DOC : k * DOC + DOC], 0.0)
            all_ref[k * TILES + t : k * TILES + t + 1, :] = jnp.sum(mine, axis=0, keepdims=True)
        all_ref[2 * TILES + t : 2 * TILES + t + 1, :] = extra_ref[2, r, g : g + 1, :]
    all_ref[62:64, :] = jnp.zeros((2, 128), F32)
    for c in range(FEATS):
        all_ref[60:62, :] = bits_ref[2 * c : 2 * c + 2, :]
        out_ref[c] = all_ref[...].astype(BF16)


def histogram_kernel(col_ref, shares_ref, bins_ref, parent_ref, out_ref, node_ref, sums_ref, vals_ref, acc_ref):
    sums = shares_ref[0].astype(F32)
    for c in range(1, FEATS):
        sums = sums + shares_ref[c].astype(F32)
    sums_ref[...] = sums
    node_ref[...] = 2 * parent_ref[pl.ds(2 * col_ref[0], 2), :] + sums_ref[60:62, :].astype(I32)

    child = (iota((16, 128), 0) >> 3).astype(F32)
    for t in range(TILES):
        bit = sums_ref[2 * TILES + t : 2 * TILES + t + 1, :]
        for k in range(2):
            value = sums_ref[k * TILES + t : k * TILES + t + 1, :]
            vals_ref[k * 16 : k * 16 + 16, t * 128 : t * 128 + 128] = jnp.where(
                child == bit, value, 0.0
            ).astype(BF16)

    vals = [vals_ref[0:16, :], vals_ref[16:32, :]]
    zero = jnp.zeros((16, TAKEN), BF16)
    one = jnp.ones((16, TAKEN), BF16)
    odd = iota((16, TAKEN), 0) >> 3
    row = iota((256, 256), 0)
    lane = iota((256, 256), 1)
    own = (row & 7) == (lane & 7)
    fold = as_hot((row >> 3) == (lane & 31))
    block = iota((32, 256), 1) >> 5
    for g in range(SPAN // 8):
        bins = bins_ref[g // 2 * 16 : g // 2 * 16 + 16, :].astype(F32)
        bins = bins[g % 2 * 8 : g % 2 * 8 + 8, :]
        high = jnp.floor(bins * (1.0 / 32.0))
        low = bins - high * 32.0
        high = jnp.concatenate([high, high], axis=0).astype(BF16)
        low = (jnp.concatenate([low, low], axis=0) - odd.astype(F32)).astype(BF16)
        tall = []
        for h in range(8):
            hit = high == jnp.array(h, BF16)
            tall += [jnp.where(hit, v, zero) for v in vals]
        flat = [jnp.where(low == jnp.array(2 * l, BF16), one, zero) for l in range(16)]
        acc_ref[g * 256 : g * 256 + 256, :] = nt(jnp.concatenate(tall, axis=0), jnp.concatenate(flat, axis=0))
    two = jnp.concatenate([fold, fold], axis=0)
    for g in range(SPAN // 8):
        acc = jnp.where(own, acc_ref[g * 256 : g * 256 + 256, :], 0.0)
        top = acc.astype(BF16)
        rest = (acc - top.astype(F32)).astype(BF16)
        wide = nn(jnp.concatenate([top, rest], axis=1), two)
        total = jnp.zeros((32, 256), F32)
        for h in range(8):
            total = jnp.where(block == h, wide[h * 32 : h * 32 + 32, :], total)
        for k in range(4):
            out_ref[k, g * 8 : g * 8 + 8, :] = total[k * 8 : k * 8 + 8, :].astype(BF16)


SMEM = pl.BlockSpec(memory_space=pltpu.SMEM)
VMEM = pl.BlockSpec(memory_space=pltpu.VMEM)


def call(kernel, ins, outs, scratch=(), **more):
    return pl.pallas_call(
        kernel,
        out_shape=[pltpu.VMEM(s, d) for s, d in outs],
        in_specs=list(ins),
        out_specs=[VMEM] * len(outs),
        scratch_shapes=list(scratch),
        **more,
    )


def near(x):
    return pltpu.with_memory_space_constraint(x, pltpu.VMEM)


def exchange(x, **more):
    return lax.all_to_all(x, "rows", split_axis=0, concat_axis=0, tiled=True, **more)


def local(
    scores, weights, labels, owner_row, owner_slot, query_len, bin_index, parent, split_feat, split_thr
):
    column = lax.axis_index("feat").astype(I32).reshape(1)
    classes = [[32 * h + 2 * i + k for i in range(PEERS)] for h in range(2) for k in range(2)]
    quads = [[2 * p, 2 * p + 1, 32 + 2 * p, 33 + 2 * p] for p in range(PARENTS)]

    def line(x):
        return x.reshape(1, DOC)

    (outbound,) = call(send_kernel, [VMEM] * 5, [((ROWS, 1, 128), F32)])(
        line(scores), line(weights), line(labels), line(owner_row), line(owner_slot)
    )
    inbound = exchange(outbound)
    sorted_docs, bits = call(
        sort_kernel,
        [SMEM] * 3 + [VMEM] * 4,
        [((PEERS, CHUNK, 128), BF16), ((1, GROUP), F32)],
        [pltpu.VMEM((512, 512), BF16), pltpu.VMEM((80, GROUP), BF16), pltpu.VMEM((512, 128), BF16)],
    )(
        split_feat,
        split_thr,
        column,
        parent.reshape(1, GROUP),
        bin_index,
        line(owner_row),
        line(owner_slot),
    )
    taken = exchange(sorted_docs, axis_index_groups=classes)
    (spread,) = call(owner_kernel, [SMEM, VMEM], [((ROWS, 2, DOC), BF16)])(query_len, near(inbound))
    grads = exchange(spread)
    bins, extra = call(
        open_kernel, [VMEM], [((SPAN, TAKEN), BF16), ((3, PEERS // 4, 8, 128), F32)]
    )(near(taken))
    (share,) = call(
        pick_kernel, [VMEM] * 3, [((FEATS, SHARE, 128), BF16)], [pltpu.VMEM((SHARE, 128), F32)]
    )(near(grads), near(extra), near(bits.reshape(16, 128)))
    shares = lax.all_to_all(share, "feat", split_axis=0, concat_axis=0, tiled=True)
    rows, new_node = call(
        histogram_kernel,
        [SMEM] + [VMEM] * 3,
        [((4, SPAN, BINS), BF16), ((2, 128), I32)],
        [
            pltpu.VMEM((SHARE, 128), F32),
            pltpu.VMEM((32, TAKEN), BF16),
            pltpu.VMEM((SPAN // 8 * 256, 256), F32),
        ],
    )(column, near(shares), near(bins), parent.reshape(16, 128))
    came = exchange(rows, axis_index_groups=quads)
    return (jnp.sum(came.astype(F32), axis=0, keepdims=True), new_node.reshape(DOC))


def solution(mesh):
    docs = P(("rows", "feat"))
    placed = (docs,) * 5 + (P(("rows", "feat"), None), P("feat", "rows"), P("rows"), P(), P())
    return jax.shard_map(
        local,
        mesh=mesh,
        in_specs=placed,
        out_specs=(P("rows", "feat", None), docs),
        check_vma=False,
    )
```

```python
import functools

import jax
import jax.numpy as jnp
from jax import lax
from jax.experimental import pallas as pl
from jax.experimental.pallas import tpu as pltpu
from jax.sharding import PartitionSpec as P

BINS = 256
NODES = 32
QMAX = 128
PARENTS = 16
ROWS = 64
FEATS = 8
DOC = 256
GROUP = FEATS * DOC
SPAN = 64
CAP = 160
SLOTS = PARENTS * CAP
POS = 8
PEERS = 16
TAKEN = PEERS * CAP
TILES = TAKEN // 128
CHUNK = 88
SHARE = 64

SCORE_UP = 2.0**40

F32 = jnp.float32
BF16 = jnp.bfloat16
I32 = jnp.int32


def iota(shape, dim):
    return lax.broadcasted_iota(I32, shape, dim)


def nt(a, b):
    return lax.dot_general(a, b, (((1,), (1,)), ((), ())), preferred_element_type=F32)


def nn(a, b):
    return jnp.dot(a, b, preferred_element_type=F32)


def as_hot(mask):
    return jnp.where(mask, 1.0, 0.0).astype(BF16)


def three_parts(x):
    top = x.astype(BF16).astype(F32)
    rest = x - top
    middle = rest.astype(BF16).astype(F32)
    return top, middle, rest - middle


def swap_matrix():
    row = iota((512, 1), 0)
    goal = ((row >> 5) & 3) * 128 + (row >> 7) * 32 + (row & 31)
    return as_hot(goal == iota((512, 512), 1))


def earlier_matrix():
    return as_hot(iota((DOC, DOC), 0) < iota((DOC, DOC), 1))


def stack_rows(rows, height, width):
    place = iota((height, width), 0)
    out = jnp.zeros((height, width), F32)
    for at, row in enumerate(rows):
        out = jnp.where(place == at, row, out)
    return out


def send_kernel(score_ref, weight_ref, label_ref, owner_ref, slot_ref, out_ref):
    owner = owner_ref[...]
    hot = jnp.where(iota((ROWS, DOC), 0) == owner, 1.0, 0.0)
    before = nn(hot.astype(BF16), earlier_matrix())
    place = jnp.sum(hot * before, axis=0, keepdims=True)
    rows = [
        *three_parts(score_ref[...] * SCORE_UP),
        *three_parts(weight_ref[...]),
        slot_ref[...].astype(F32) + 1.0,
        label_ref[...].astype(F32),
    ]
    values = stack_rows(rows, 16, DOC)
    tiled = jnp.concatenate([values] * POS, axis=0)
    group = iota((16 * POS, DOC), 0) >> 4
    total = jnp.zeros((ROWS, 128), F32)
    for pos in range(POS):
        here = jnp.where(place == float(pos), hot, 0.0).astype(BF16)
        total += nt(here, jnp.where(group == pos, tiled, 0.0).astype(BF16))
    out_ref[:, 0, :] = total


def owner_kernel(len_ref, in_ref, out_ref):
    data = in_ref[:, 0, :]
    turned = jnp.transpose(data).astype(BF16)
    lane = iota((ROWS, DOC), 1).astype(F32) + 1.0
    table = jnp.zeros((16, DOC), F32)
    for pos in range(POS):
        hot = as_hot(data[:, pos * 16 + 6 : pos * 16 + 7] == lane)
        table += nn(turned[pos * 16 : pos * 16 + 16, :], hot)
    same = as_hot(iota((DOC, DOC), 0) == iota((DOC, DOC), 1))
    upright = nt(same, table.astype(BF16))
    s_j = (table[0:1] + table[1:2] + table[2:3]) * (1.0 / SCORE_UP)
    w_j = table[3:4] + table[4:5] + table[5:6]
    l_j = table[7:8]
    s_i = (upright[:, 0:1] + upright[:, 1:2] + upright[:, 2:3]) * (1.0 / SCORE_UP)
    w_i = upright[:, 3:4] + upright[:, 4:5] + upright[:, 5:6]
    l_i = upright[:, 7:8]

    ends = []
    total = 0
    for q in range(3):
        total = total + len_ref[0, q]
        ends.append(total)

    def query_of(at):
        return sum([(at >= end).astype(I32) for end in ends])

    def gain(label):
        return sum([jnp.where(label >= float(l), 2.0 ** (l - 1), 0.0) for l in range(1, 5)])

    row_at = iota((1, DOC), 1)
    q_j = query_of(row_at)
    q_i = query_of(iota((DOC, 1), 0))
    n_j = jnp.zeros((1, DOC), F32)
    for q in range(4):
        n_j = jnp.where(q_j == q, len_ref[0, q].astype(F32), n_j)

    case = iota((16, DOC), 0)
    level = ((case & 3) + 1).astype(F32)
    reaches = (q_j == (case >> 2)) & (l_j >= level)
    count = jnp.sum(jnp.where(reaches, 1.0, 0.0), axis=1, keepdims=True)
    spot = iota((16, QMAX), 1).astype(F32)
    step = jnp.left_shift(1, iota((16, QMAX), 0) & 3).astype(F32)
    share = jnp.where(spot < count, step * (0.6931471805599453 / jnp.log(spot + 2.0)), 0.0)
    share = jnp.sum(share, axis=1, keepdims=True)
    ideal = jnp.sum(jnp.where(q_j == (case >> 2), share, 0.0), axis=0, keepdims=True)
    inverse = 1.0 / jnp.maximum(ideal, 1.0)

    mate = q_i == q_j
    earlier = iota((DOC, DOC), 1) < iota((DOC, DOC), 0)
    above = mate & ((s_j > s_i) | ((s_j == s_i) & earlier))
    above = jnp.where(above, 1.0, 0.0)
    rank_i = 1.0 + jnp.sum(above, axis=1, keepdims=True)
    rank_j = n_j - jnp.sum(above, axis=0, keepdims=True)
    disc_i = 0.6931471805599453 / jnp.log(1.0 + rank_i)
    disc_j = 0.6931471805599453 / jnp.log(1.0 + rank_j)
    step_gain = gain(l_i) - gain(l_j)
    odds = jnp.exp(s_i - s_j)
    miss = 1.0 / (1.0 + odds)
    swap = jnp.where(mate, jnp.abs(disc_i - disc_j) * w_i, 0.0) * miss
    push = swap * step_gain * jnp.where(step_gain > 0.0, 1.0, odds)
    bend = swap * jnp.abs(step_gain) * (odds * miss)
    scale = w_j * inverse
    grad = jnp.sum(push, axis=0, keepdims=True) * scale
    hess = jnp.sum(bend, axis=0, keepdims=True) * scale
    both = jnp.concatenate([grad, hess], axis=0).astype(BF16)
    for r in range(ROWS):
        out_ref[r] = both


def sort_kernel(
    feat_ref,
    thr_ref,
    col_ref,
    parent_ref,
    folded_ref,
    bins_ref,
    owner_ref,
    slot_ref,
    out_ref,
    bits_ref,
    own_ref,
    fold_ref,
    left_ref,
    tail_ref,
):
    column = col_ref[0]
    own_ref[...] = folded_ref[pl.ds(2 * column, 2), :]
    parent = parent_ref[...]
    hot = jnp.where(iota((PARENTS, GROUP), 0) == parent, 1.0, 0.0)
    hot_b = hot.astype(BF16)
    earlier = earlier_matrix()
    carry = jnp.zeros((PARENTS, 1), F32)
    ranks = []
    for block in range(FEATS):
        part = hot[:, block * DOC : (block + 1) * DOC]
        before = nn(hot_b[:, block * DOC : (block + 1) * DOC], earlier) + carry
        ranks.append(jnp.sum(part * before, axis=0, keepdims=True))
        carry = carry + jnp.sum(part, axis=1, keepdims=True)
    rank = jnp.concatenate(ranks, axis=1)

    bits = jnp.zeros((1, GROUP), F32)
    for p in range(PARENTS):
        at = feat_ref[p] - column * SPAN
        here = jnp.where((at >= 0) & (at < SPAN), 1.0, 0.0)
        row = bins_ref[pl.ds(jnp.clip(at, 0, SPAN - 1), 1), :]
        right = (parent == p) & (row > thr_ref[p])
        bits = bits + jnp.where(right, here, 0.0)
    bits_ref[...] = bits

    own = (iota((1, GROUP), 1) >> 8) == column
    owner = jnp.concatenate([owner_ref[...].astype(F32) + 1.0] * FEATS, axis=1)
    slot = jnp.concatenate([slot_ref[...].astype(F32)] * FEATS, axis=1)
    left_ref[0:SPAN, :] = bins_ref[...].astype(F32).astype(BF16)
    extra = [jnp.where(own, owner, 0.0), jnp.where(own, slot, 0.0), bits]
    left_ref[SPAN : SPAN + 16, :] = stack_rows(extra, 16, GROUP).astype(BF16)

    left = left_ref[...]
    pick = as_hot(iota((CAP, GROUP), 0).astype(F32) == rank)
    each = jnp.concatenate([left * hot_b[p : p + 1, :] for p in range(PARENTS)], axis=0)
    gathered = nt(each, pick)
    for p in range(PARENTS):
        got = gathered[p * 80 : p * 80 + 80, :]
        low = got.astype(BF16)
        for q in range(4):
            lanes = slice(q * 128, q * 128 + 128)
            rows = slice(q * 16, q * 16 + 16)
            fold_ref[p * 16 : p * 16 + 16, lanes] = low[rows, 0:128]
            ext = jnp.broadcast_to(got[SPAN + q : SPAN + q + 1, :], (16, CAP)).astype(BF16)
            fold_ref[256 + p * 16 : 272 + p * 16, lanes] = ext[:, 0:128]
            tail_ref[p * 16 : p * 16 + 16, q * 32 : q * 32 + 32] = low[rows, 128:160]
            tail_ref[256 + p * 16 : 272 + p * 16, q * 32 : q * 32 + 32] = ext[:, 128:160]
    folded = nn(fold_ref[...], swap_matrix())
    which = iota((16, 128), 0)
    for p in range(PARENTS):
        for g in range(4):
            out_ref[p, g * 16 : g * 16 + 16, :] = folded[
                p * 16 : p * 16 + 16, g * 128 : g * 128 + 128
            ].astype(BF16)
        out_ref[p, 64:80, :] = tail_ref[p * 16 : p * 16 + 16, :]
        last = tail_ref[256 + p * 16 : 272 + p * 16, :].astype(F32)
        for g in range(4):
            last = jnp.where(which == g, folded[256 + p * 16 : 272 + p * 16, g * 128 : g * 128 + 128], last)
        out_ref[p, 80:88, :] = last[0:8].astype(BF16)


def open_kernel(in_ref, bins_ref, extra_ref):
    swap = swap_matrix()
    for r in range(PEERS // 4):
        four = jnp.concatenate([in_ref[4 * r + a] for a in range(4)], axis=1)
        flat = nn(four, swap)
        for g in range(5):
            t = r * 5 + g
            for q in range(4):
                bins_ref[q * 16 : q * 16 + 16, t * 128 : t * 128 + 128] = flat[
                    g * 16 : g * 16 + 16, q * 128 : q * 128 + 128
                ].astype(BF16)
        for q in range(3):
            extra_ref[q, r] = flat[80:88, q * 128 : q * 128 + 128]


def pick_kernel(grads_ref, extra_ref, bits_ref, out_ref, all_ref):
    turned = jnp.concatenate([jnp.transpose(grads_ref[:, k, :].astype(F32)) for k in range(2)], axis=0)
    turned = turned.astype(BF16)
    owner_line = (iota((ROWS, 128), 0) + 1).astype(F32)
    slot_line = iota((DOC, 128), 0).astype(F32)
    for t in range(TILES):
        r, g = divmod(t, 5)
        owner = extra_ref[0, r, g : g + 1, :]
        slot = extra_ref[1, r, g : g + 1, :]
        from_owner = nn(turned, as_hot(owner_line == owner))
        hit = slot_line == slot
        for k in range(2):
            mine = jnp.where(hit, from_owner[k * DOC : k * DOC + DOC], 0.0)
            all_ref[k * TILES + t : k * TILES + t + 1, :] = jnp.sum(mine, axis=0, keepdims=True)
        all_ref[2 * TILES + t : 2 * TILES + t + 1, :] = extra_ref[2, r, g : g + 1, :]
    all_ref[62:64, :] = jnp.zeros((2, 128), F32)
    for c in range(FEATS):
        all_ref[60:62, :] = bits_ref[2 * c : 2 * c + 2, :]
        out_ref[c] = all_ref[...].astype(BF16)


def histogram_kernel(shares_ref, bins_ref, parent_ref, out_ref, node_ref, sums_ref, vals_ref, acc_ref):
    sums = shares_ref[0].astype(F32)
    for c in range(1, FEATS):
        sums = sums + shares_ref[c].astype(F32)
    sums_ref[...] = sums
    node_ref[...] = 2 * parent_ref[...] + sums_ref[60:62, :].astype(I32)

    child = (iota((16, 128), 0) >> 3).astype(F32)
    for t in range(TILES):
        bit = sums_ref[2 * TILES + t : 2 * TILES + t + 1, :]
        for k in range(2):
            value = sums_ref[k * TILES + t : k * TILES + t + 1, :]
            vals_ref[k * 16 : k * 16 + 16, t * 128 : t * 128 + 128] = jnp.where(
                child == bit, value, 0.0
            ).astype(BF16)

    vals = [vals_ref[0:16, :], vals_ref[16:32, :]]
    zero = jnp.zeros((16, TAKEN), BF16)
    one = jnp.ones((16, TAKEN), BF16)
    odd = iota((16, TAKEN), 0) >> 3
    row = iota((256, 256), 0)
    lane = iota((256, 256), 1)
    own = (row & 7) == (lane & 7)
    fold = as_hot((row >> 3) == (lane & 31))
    block = iota((32, 256), 1) >> 5
    for g in range(SPAN // 8):
        bins = bins_ref[g // 2 * 16 : g // 2 * 16 + 16, :].astype(F32)
        bins = bins[g % 2 * 8 : g % 2 * 8 + 8, :]
        high = jnp.floor(bins * (1.0 / 32.0))
        low = bins - high * 32.0
        high = jnp.concatenate([high, high], axis=0).astype(BF16)
        low = (jnp.concatenate([low, low], axis=0) - odd.astype(F32)).astype(BF16)
        tall = []
        for h in range(8):
            hit = high == jnp.array(h, BF16)
            tall += [jnp.where(hit, v, zero) for v in vals]
        flat = [jnp.where(low == jnp.array(2 * l, BF16), one, zero) for l in range(16)]
        acc_ref[g * 256 : g * 256 + 256, :] = nt(jnp.concatenate(tall, axis=0), jnp.concatenate(flat, axis=0))
    two = jnp.concatenate([fold, fold], axis=0)
    for g in range(SPAN // 8):
        acc = jnp.where(own, acc_ref[g * 256 : g * 256 + 256, :], 0.0)
        top = acc.astype(BF16)
        rest = (acc - top.astype(F32)).astype(BF16)
        wide = nn(jnp.concatenate([top, rest], axis=1), two)
        total = jnp.zeros((32, 256), F32)
        for h in range(8):
            total = jnp.where(block == h, wide[h * 32 : h * 32 + 32, :], total)
        for k in range(4):
            out_ref[k, g * 8 : g * 8 + 8, :] = total[k * 8 : k * 8 + 8, :].astype(BF16)


SMEM = pl.BlockSpec(memory_space=pltpu.SMEM)
VMEM = pl.BlockSpec(memory_space=pltpu.VMEM)


def call(kernel, ins, outs, scratch=(), **more):
    return pl.pallas_call(
        kernel,
        out_shape=[pltpu.VMEM(s, d) for s, d in outs],
        in_specs=list(ins),
        out_specs=[VMEM] * len(outs),
        scratch_shapes=list(scratch),
        **more,
    )


def near(x):
    return pltpu.with_memory_space_constraint(x, pltpu.VMEM)


def exchange(x, **more):
    return lax.all_to_all(x, "rows", split_axis=0, concat_axis=0, tiled=True, **more)


def local(
    scores, weights, labels, owner_row, owner_slot, query_len, bin_index, parent, split_feat, split_thr
):
    column = lax.axis_index("feat").astype(I32).reshape(1)
    classes = [[32 * h + 2 * i + k for i in range(PEERS)] for h in range(2) for k in range(2)]
    quads = [[2 * p, 2 * p + 1, 32 + 2 * p, 33 + 2 * p] for p in range(PARENTS)]

    def line(x):
        return x.reshape(1, DOC)

    (outbound,) = call(send_kernel, [VMEM] * 5, [((ROWS, 1, 128), F32)])(
        line(scores), line(weights), line(labels), line(owner_row), line(owner_slot)
    )
    inbound = exchange(outbound)
    sorted_docs, bits, own_parent = call(
        sort_kernel,
        [SMEM] * 3 + [VMEM] * 5,
        [((PEERS, CHUNK, 128), BF16), ((1, GROUP), F32), ((2, 128), I32)],
        [pltpu.VMEM((512, 512), BF16), pltpu.VMEM((80, GROUP), BF16), pltpu.VMEM((512, 128), BF16)],
    )(
        split_feat,
        split_thr,
        column,
        parent.reshape(1, GROUP),
        parent.reshape(16, 128),
        bin_index,
        line(owner_row),
        line(owner_slot),
    )
    taken = exchange(sorted_docs, axis_index_groups=classes)
    (spread,) = call(owner_kernel, [SMEM, VMEM], [((ROWS, 2, DOC), BF16)])(query_len, near(inbound))
    grads = exchange(spread)
    bins, extra = call(
        open_kernel, [VMEM], [((SPAN, TAKEN), BF16), ((3, PEERS // 4, 8, 128), F32)]
    )(near(taken))
    (share,) = call(
        pick_kernel, [VMEM] * 3, [((FEATS, SHARE, 128), BF16)], [pltpu.VMEM((SHARE, 128), F32)]
    )(near(grads), near(extra), near(bits.reshape(16, 128)))
    shares = lax.all_to_all(share, "feat", split_axis=0, concat_axis=0, tiled=True)
    rows, new_node = call(
        histogram_kernel,
        [VMEM] * 3,
        [((4, SPAN, BINS), BF16), ((2, 128), I32)],
        [
            pltpu.VMEM((SHARE, 128), F32),
            pltpu.VMEM((32, TAKEN), BF16),
            pltpu.VMEM((SPAN // 8 * 256, 256), F32),
        ],
    )(near(shares), near(bins), near(own_parent))
    came = exchange(rows, axis_index_groups=quads)
    return (jnp.sum(came.astype(F32), axis=0, keepdims=True), new_node.reshape(DOC))


def solution(mesh):
    docs = P(("rows", "feat"))
    placed = (docs,) * 5 + (P(("rows", "feat"), None), P("feat", "rows"), P("rows"), P(), P())
    return jax.shard_map(
        local,
        mesh=mesh,
        in_specs=placed,
        out_specs=(P("rows", "feat", None), docs),
        check_vma=False,
    )
```

```python
import functools

import jax
import jax.numpy as jnp
from jax import lax
from jax.experimental import pallas as pl
from jax.experimental.pallas import tpu as pltpu
from jax.sharding import PartitionSpec as P

BINS = 256
NODES = 32
QMAX = 128
PARENTS = 16
ROWS = 64
FEATS = 8
DOC = 256
GROUP = FEATS * DOC
SPAN = 64
CAP = 160
SLOTS = PARENTS * CAP
POS = 8
PEERS = 16
TAKEN = PEERS * CAP
TILES = TAKEN // 128
CHUNK = 88
SHARE = 64

SCORE_UP = 2.0**40

F32 = jnp.float32
BF16 = jnp.bfloat16
I32 = jnp.int32


def iota(shape, dim):
    return lax.broadcasted_iota(I32, shape, dim)


def nt(a, b):
    return lax.dot_general(a, b, (((1,), (1,)), ((), ())), preferred_element_type=F32)


def nn(a, b):
    return jnp.dot(a, b, preferred_element_type=F32)


def as_hot(mask):
    return jnp.where(mask, 1.0, 0.0).astype(BF16)


def three_parts(x):
    top = x.astype(BF16).astype(F32)
    rest = x - top
    middle = rest.astype(BF16).astype(F32)
    return top, middle, rest - middle


def swap_matrix():
    row = iota((512, 1), 0)
    goal = ((row >> 5) & 3) * 128 + (row >> 7) * 32 + (row & 31)
    return as_hot(goal == iota((512, 512), 1))


def earlier_matrix():
    return as_hot(iota((DOC, DOC), 0) < iota((DOC, DOC), 1))


def stack_rows(rows, height, width):
    place = iota((height, width), 0)
    out = jnp.zeros((height, width), F32)
    for at, row in enumerate(rows):
        out = jnp.where(place == at, row, out)
    return out


def send_kernel(score_ref, weight_ref, label_ref, owner_ref, slot_ref, out_ref):
    owner = owner_ref[...]
    hot = jnp.where(iota((ROWS, DOC), 0) == owner, 1.0, 0.0)
    before = nn(hot.astype(BF16), earlier_matrix())
    place = jnp.sum(hot * before, axis=0, keepdims=True)
    rows = [
        *three_parts(score_ref[...] * SCORE_UP),
        *three_parts(weight_ref[...]),
        slot_ref[...].astype(F32) + 1.0,
        label_ref[...].astype(F32),
    ]
    values = stack_rows(rows, 16, DOC)
    tiled = jnp.concatenate([values] * POS, axis=0)
    group = iota((16 * POS, DOC), 0) >> 4
    total = jnp.zeros((ROWS, 128), F32)
    for pos in range(POS):
        here = jnp.where(place == float(pos), hot, 0.0).astype(BF16)
        total += nt(here, jnp.where(group == pos, tiled, 0.0).astype(BF16))
    out_ref[:, 0, :] = total


def owner_kernel(len_ref, in_ref, out_ref):
    data = in_ref[:, 0, :]
    turned = jnp.transpose(data).astype(BF16)
    lane = iota((ROWS, DOC), 1).astype(F32) + 1.0
    table = jnp.zeros((16, DOC), F32)
    for pos in range(POS):
        hot = as_hot(data[:, pos * 16 + 6 : pos * 16 + 7] == lane)
        table += nn(turned[pos * 16 : pos * 16 + 16, :], hot)
    same = as_hot(iota((DOC, DOC), 0) == iota((DOC, DOC), 1))
    upright = nt(same, table.astype(BF16))
    s_j = (table[0:1] + table[1:2] + table[2:3]) * (1.0 / SCORE_UP)
    w_j = table[3:4] + table[4:5] + table[5:6]
    l_j = table[7:8]
    s_i = (upright[:, 0:1] + upright[:, 1:2] + upright[:, 2:3]) * (1.0 / SCORE_UP)
    w_i = upright[:, 3:4] + upright[:, 4:5] + upright[:, 5:6]
    l_i = upright[:, 7:8]

    ends = []
    total = 0
    for q in range(3):
        total = total + len_ref[0, q]
        ends.append(total)

    def query_of(at):
        return sum([(at >= end).astype(I32) for end in ends])

    def gain(label):
        return sum([jnp.where(label >= float(l), 2.0 ** (l - 1), 0.0) for l in range(1, 5)])

    row_at = iota((1, DOC), 1)
    q_j = query_of(row_at)
    q_i = query_of(iota((DOC, 1), 0))
    n_j = jnp.zeros((1, DOC), F32)
    for q in range(4):
        n_j = jnp.where(q_j == q, len_ref[0, q].astype(F32), n_j)

    case = iota((16, DOC), 0)
    level = ((case & 3) + 1).astype(F32)
    reaches = (q_j == (case >> 2)) & (l_j >= level)
    count = jnp.sum(jnp.where(reaches, 1.0, 0.0), axis=1, keepdims=True)
    spot = iota((16, QMAX), 1).astype(F32)
    step = jnp.left_shift(1, iota((16, QMAX), 0) & 3).astype(F32)
    share = jnp.where(spot < count, step * (0.6931471805599453 / jnp.log(spot + 2.0)), 0.0)
    share = jnp.sum(share, axis=1, keepdims=True)
    ideal = jnp.sum(jnp.where(q_j == (case >> 2), share, 0.0), axis=0, keepdims=True)
    inverse = 1.0 / jnp.maximum(ideal, 1.0)

    mate = q_i == q_j
    earlier = iota((DOC, DOC), 1) < iota((DOC, DOC), 0)
    above = mate & ((s_j > s_i) | ((s_j == s_i) & earlier))
    above = jnp.where(above, 1.0, 0.0)
    rank_i = 1.0 + jnp.sum(above, axis=1, keepdims=True)
    rank_j = n_j - jnp.sum(above, axis=0, keepdims=True)
    disc_i = 0.6931471805599453 / jnp.log(1.0 + rank_i)
    disc_j = 0.6931471805599453 / jnp.log(1.0 + rank_j)
    step_gain = gain(l_i) - gain(l_j)
    odds = jnp.exp(s_i - s_j)
    miss = 1.0 / (1.0 + odds)
    swap = jnp.where(mate, jnp.abs(disc_i - disc_j) * w_i, 0.0) * miss
    push = swap * step_gain * jnp.where(step_gain > 0.0, 1.0, odds)
    bend = swap * jnp.abs(step_gain) * (odds * miss)
    scale = w_j * inverse
    grad = jnp.sum(push, axis=0, keepdims=True) * scale
    hess = jnp.sum(bend, axis=0, keepdims=True) * scale
    both = jnp.concatenate([grad, hess], axis=0).astype(BF16)
    for r in range(ROWS):
        out_ref[r] = both


def sort_kernel(
    feat_ref,
    thr_ref,
    col_ref,
    parent_ref,
    folded_ref,
    bins_ref,
    owner_ref,
    slot_ref,
    out_ref,
    bits_ref,
    own_ref,
    fold_ref,
    left_ref,
    tail_ref,
):
    column = col_ref[0]
    own = folded_ref[pl.ds(2 * column, 2), :]
    own_ref[...] = jnp.concatenate([own[0:1], own[1:2]], axis=1)
    parent = parent_ref[...]
    hot = jnp.where(iota((PARENTS, GROUP), 0) == parent, 1.0, 0.0)
    hot_b = hot.astype(BF16)
    earlier = earlier_matrix()
    carry = jnp.zeros((PARENTS, 1), F32)
    ranks = []
    for block in range(FEATS):
        part = hot[:, block * DOC : (block + 1) * DOC]
        before = nn(hot_b[:, block * DOC : (block + 1) * DOC], earlier) + carry
        ranks.append(jnp.sum(part * before, axis=0, keepdims=True))
        carry = carry + jnp.sum(part, axis=1, keepdims=True)
    rank = jnp.concatenate(ranks, axis=1)

    bits = jnp.zeros((1, GROUP), F32)
    for p in range(PARENTS):
        at = feat_ref[p] - column * SPAN
        here = jnp.where((at >= 0) & (at < SPAN), 1.0, 0.0)
        row = bins_ref[pl.ds(jnp.clip(at, 0, SPAN - 1), 1), :]
        right = (parent == p) & (row > thr_ref[p])
        bits = bits + jnp.where(right, here, 0.0)
    bits_ref[...] = bits

    own = (iota((1, GROUP), 1) >> 8) == column
    owner = jnp.concatenate([owner_ref[...].astype(F32) + 1.0] * FEATS, axis=1)
    slot = jnp.concatenate([slot_ref[...].astype(F32)] * FEATS, axis=1)
    left_ref[0:SPAN, :] = bins_ref[...].astype(F32).astype(BF16)
    extra = [jnp.where(own, owner, 0.0), jnp.where(own, slot, 0.0), bits]
    left_ref[SPAN : SPAN + 16, :] = stack_rows(extra, 16, GROUP).astype(BF16)

    left = left_ref[...]
    pick = as_hot(iota((CAP, GROUP), 0).astype(F32) == rank)
    each = jnp.concatenate([left * hot_b[p : p + 1, :] for p in range(PARENTS)], axis=0)
    gathered = nt(each, pick)
    for p in range(PARENTS):
        got = gathered[p * 80 : p * 80 + 80, :]
        low = got.astype(BF16)
        for q in range(4):
            lanes = slice(q * 128, q * 128 + 128)
            rows = slice(q * 16, q * 16 + 16)
            fold_ref[p * 16 : p * 16 + 16, lanes] = low[rows, 0:128]
            ext = jnp.broadcast_to(got[SPAN + q : SPAN + q + 1, :], (16, CAP)).astype(BF16)
            fold_ref[256 + p * 16 : 272 + p * 16, lanes] = ext[:, 0:128]
            tail_ref[p * 16 : p * 16 + 16, q * 32 : q * 32 + 32] = low[rows, 128:160]
            tail_ref[256 + p * 16 : 272 + p * 16, q * 32 : q * 32 + 32] = ext[:, 128:160]
    folded = nn(fold_ref[...], swap_matrix())
    which = iota((16, 128), 0)
    for p in range(PARENTS):
        for g in range(4):
            out_ref[p, g * 16 : g * 16 + 16, :] = folded[
                p * 16 : p * 16 + 16, g * 128 : g * 128 + 128
            ].astype(BF16)
        out_ref[p, 64:80, :] = tail_ref[p * 16 : p * 16 + 16, :]
        last = tail_ref[256 + p * 16 : 272 + p * 16, :].astype(F32)
        for g in range(4):
            last = jnp.where(which == g, folded[256 + p * 16 : 272 + p * 16, g * 128 : g * 128 + 128], last)
        out_ref[p, 80:88, :] = last[0:8].astype(BF16)


def open_kernel(in_ref, bins_ref, extra_ref):
    swap = swap_matrix()
    for r in range(PEERS // 4):
        four = jnp.concatenate([in_ref[4 * r + a] for a in range(4)], axis=1)
        flat = nn(four, swap)
        for g in range(5):
            t = r * 5 + g
            for q in range(4):
                bins_ref[q * 16 : q * 16 + 16, t * 128 : t * 128 + 128] = flat[
                    g * 16 : g * 16 + 16, q * 128 : q * 128 + 128
                ].astype(BF16)
        for q in range(3):
            extra_ref[q, r] = flat[80:88, q * 128 : q * 128 + 128]


def pick_kernel(grads_ref, extra_ref, bits_ref, out_ref, all_ref):
    turned = jnp.concatenate([jnp.transpose(grads_ref[:, k, :].astype(F32)) for k in range(2)], axis=0)
    turned = turned.astype(BF16)
    owner_line = (iota((ROWS, 128), 0) + 1).astype(F32)
    slot_line = iota((DOC, 128), 0).astype(F32)
    for t in range(TILES):
        r, g = divmod(t, 5)
        owner = extra_ref[0, r, g : g + 1, :]
        slot = extra_ref[1, r, g : g + 1, :]
        from_owner = nn(turned, as_hot(owner_line == owner))
        hit = slot_line == slot
        for k in range(2):
            mine = jnp.where(hit, from_owner[k * DOC : k * DOC + DOC], 0.0)
            all_ref[k * TILES + t : k * TILES + t + 1, :] = jnp.sum(mine, axis=0, keepdims=True)
        all_ref[2 * TILES + t : 2 * TILES + t + 1, :] = extra_ref[2, r, g : g + 1, :]
    all_ref[62:64, :] = jnp.zeros((2, 128), F32)
    for c in range(FEATS):
        all_ref[60:62, :] = bits_ref[2 * c : 2 * c + 2, :]
        out_ref[c] = all_ref[...].astype(BF16)


def histogram_kernel(shares_ref, bins_ref, parent_ref, out_ref, node_ref, sums_ref, vals_ref, acc_ref):
    sums = shares_ref[0].astype(F32)
    for c in range(1, FEATS):
        sums = sums + shares_ref[c].astype(F32)
    sums_ref[...] = sums
    right = jnp.concatenate([sums_ref[60:61, :], sums_ref[61:62, :]], axis=1)
    node_ref[...] = 2 * parent_ref[...] + right.astype(I32)

    child = (iota((16, 128), 0) >> 3).astype(F32)
    for t in range(TILES):
        bit = sums_ref[2 * TILES + t : 2 * TILES + t + 1, :]
        for k in range(2):
            value = sums_ref[k * TILES + t : k * TILES + t + 1, :]
            vals_ref[k * 16 : k * 16 + 16, t * 128 : t * 128 + 128] = jnp.where(
                child == bit, value, 0.0
            ).astype(BF16)

    vals = [vals_ref[0:16, :], vals_ref[16:32, :]]
    zero = jnp.zeros((16, TAKEN), BF16)
    one = jnp.ones((16, TAKEN), BF16)
    odd = iota((16, TAKEN), 0) >> 3
    row = iota((256, 256), 0)
    lane = iota((256, 256), 1)
    own = (row & 7) == (lane & 7)
    fold = as_hot((row >> 3) == (lane & 31))
    block = iota((32, 256), 1) >> 5
    for g in range(SPAN // 8):
        bins = bins_ref[g // 2 * 16 : g // 2 * 16 + 16, :].astype(F32)
        bins = bins[g % 2 * 8 : g % 2 * 8 + 8, :]
        high = jnp.floor(bins * (1.0 / 32.0))
        low = bins - high * 32.0
        high = jnp.concatenate([high, high], axis=0).astype(BF16)
        low = (jnp.concatenate([low, low], axis=0) - odd.astype(F32)).astype(BF16)
        tall = []
        for h in range(8):
            hit = high == jnp.array(h, BF16)
            tall += [jnp.where(hit, v, zero) for v in vals]
        flat = [jnp.where(low == jnp.array(2 * l, BF16), one, zero) for l in range(16)]
        acc_ref[g * 256 : g * 256 + 256, :] = nt(jnp.concatenate(tall, axis=0), jnp.concatenate(flat, axis=0))
    two = jnp.concatenate([fold, fold], axis=0)
    for g in range(SPAN // 8):
        acc = jnp.where(own, acc_ref[g * 256 : g * 256 + 256, :], 0.0)
        top = acc.astype(BF16)
        rest = (acc - top.astype(F32)).astype(BF16)
        wide = nn(jnp.concatenate([top, rest], axis=1), two)
        total = jnp.zeros((32, 256), F32)
        for h in range(8):
            total = jnp.where(block == h, wide[h * 32 : h * 32 + 32, :], total)
        for k in range(4):
            out_ref[k, g * 8 : g * 8 + 8, :] = total[k * 8 : k * 8 + 8, :].astype(BF16)


SMEM = pl.BlockSpec(memory_space=pltpu.SMEM)
VMEM = pl.BlockSpec(memory_space=pltpu.VMEM)


def call(kernel, ins, outs, scratch=(), **more):
    return pl.pallas_call(
        kernel,
        out_shape=[pltpu.VMEM(*o) if len(o) == 2 else jax.ShapeDtypeStruct(*o[:2]) for o in outs],
        in_specs=list(ins),
        out_specs=[VMEM] * len(outs),
        scratch_shapes=list(scratch),
        **more,
    )


def near(x):
    return pltpu.with_memory_space_constraint(x, pltpu.VMEM)


def exchange(x, **more):
    return lax.all_to_all(x, "rows", split_axis=0, concat_axis=0, tiled=True, **more)


def local(
    scores, weights, labels, owner_row, owner_slot, query_len, bin_index, parent, split_feat, split_thr
):
    column = lax.axis_index("feat").astype(I32).reshape(1)
    classes = [[32 * h + 2 * i + k for i in range(PEERS)] for h in range(2) for k in range(2)]
    quads = [[2 * p, 2 * p + 1, 32 + 2 * p, 33 + 2 * p] for p in range(PARENTS)]

    def line(x):
        return x.reshape(1, DOC)

    (outbound,) = call(send_kernel, [VMEM] * 5, [((ROWS, 1, 128), F32)])(
        line(scores), line(weights), line(labels), line(owner_row), line(owner_slot)
    )
    inbound = exchange(outbound)
    sorted_docs, bits, own_parent = call(
        sort_kernel,
        [SMEM] * 3 + [VMEM] * 5,
        [((PEERS, CHUNK, 128), BF16), ((1, GROUP), F32), ((1, DOC), I32)],
        [pltpu.VMEM((512, 512), BF16), pltpu.VMEM((80, GROUP), BF16), pltpu.VMEM((512, 128), BF16)],
    )(
        split_feat,
        split_thr,
        column,
        parent.reshape(1, GROUP),
        parent.reshape(16, 128),
        bin_index,
        line(owner_row),
        line(owner_slot),
    )
    (spread,) = call(owner_kernel, [SMEM, VMEM], [((ROWS, 2, DOC), BF16)])(query_len, near(inbound))
    grads = exchange(spread)
    grads, sorted_docs = lax.optimization_barrier((grads, sorted_docs))
    taken = exchange(sorted_docs, axis_index_groups=classes)
    bins, extra = call(
        open_kernel, [VMEM], [((SPAN, TAKEN), BF16), ((3, PEERS // 4, 8, 128), F32)]
    )(near(taken))
    (share,) = call(
        pick_kernel, [VMEM] * 3, [((FEATS, SHARE, 128), BF16)], [pltpu.VMEM((SHARE, 128), F32)]
    )(near(grads), near(extra), near(bits.reshape(16, 128)))
    shares = lax.all_to_all(share, "feat", split_axis=0, concat_axis=0, tiled=True)
    rows, new_node = call(
        histogram_kernel,
        [VMEM] * 3,
        [((4, SPAN, BINS), BF16), ((1, DOC), I32, "hbm")],
        [
            pltpu.VMEM((SHARE, 128), F32),
            pltpu.VMEM((32, TAKEN), BF16),
            pltpu.VMEM((SPAN // 8 * 256, 256), F32),
        ],
    )(near(shares), near(bins), near(own_parent))
    came = exchange(rows, axis_index_groups=quads)
    return (jnp.sum(came.astype(F32), axis=0, keepdims=True), new_node.reshape(DOC))


def solution(mesh):
    docs = P(("rows", "feat"))
    placed = (docs,) * 5 + (P(("rows", "feat"), None), P("feat", "rows"), P("rows"), P(), P())
    return jax.shard_map(
        local,
        mesh=mesh,
        in_specs=placed,
        out_specs=(P("rows", "feat", None), docs),
        check_vma=False,
    )
```
